128 devices in a mesh: gy: 8 (over z, x_hi), gx: 16 (over y, x_lo, core).
Axes of the slice: x: 4 (x_hi: 2, x_lo: 2; x = x_hi * 2 + x_lo), y: 4, z: 4, core: 2. Of those that a mesh axis runs over, the one named last changes fastest.
Arguments:
- tiles: bfloat16 [16384, 128, 128], P(('gy', 'gx')), may hold values from 0.19921875 to 5
- tile_dest: int32 [16384, 1], P(('gy', 'gx')), may hold values from 0 to 127, as said below
- tile_slot: int32 [16384], P(('gy', 'gx')), may hold values from 0 to 191
- psf: float32 [6, 3, 31], replicated, may hold values from 0.05 to 1
- estimate: float32 [32, 1024, 2048], P(None, 'gy', 'gx'), may hold values from 0.5 to 2
Outputs:
- restored: float32 [32, 1024, 2048], P(None, 'gy', 'gx')
The draws below stay inside these ranges and needn't reach their ends.
Inputs may be any that keep to these rules, and one draw needn't show every extreme that they name: `tile_dest`: among the 128 tiles held by one device no brick is named more than 2 times; in every draw some brick is named exactly 2 times by the tiles of every device.
All inputs are finite; a program needn't handle non-finite values.
Results may differ from the reference program's by a relative error of at most 0.00069.
Values may be sent and summed in bfloat16 or wider, within the bound.
No kernel may reach another device: no remote copies, remote signals or barrier semaphores. Data moves between devices by JAX's collectives and lax.ppermute only.
A program may use at most 192 MiB of HBM per device.

```python
import math
import jax
import jax.numpy as jnp
from jax import lax

TILE = 128
CZ = 32
VIEWS = 6
TAPS = 31
ITERS = 2
TILES_DEV = 128
HALF = 15
SLOTS = 2
TILES = 16384
NY = 1024
NX = 2048
N_GY = 8
N_GX = 16
DEVICES = 128


def draw_tile_dest(key, part):
    hottest = jax.random.randint(jax.random.fold_in(key, 7), (), 0, DEVICES)

    def holder(holder_index):
        holder_key = jax.random.fold_in(key, holder_index + 100)
        increments = jax.random.randint(jax.random.fold_in(holder_key, 1), (TILES_DEV - SLOTS,), 1, 3)
        position = jnp.cumsum(increments) - increments
        grouping = position // SLOTS
        ordering = jax.random.permutation(jax.random.fold_in(holder_key, 2), DEVICES - 1)
        picked = ordering[grouping]
        picked = picked + (picked >= hottest).astype(jnp.int32)
        return jnp.concatenate([jnp.full((SLOTS,), hottest, jnp.int32), picked.astype(jnp.int32)])
    targets = jax.vmap(holder)(jnp.arange(DEVICES))
    return targets.reshape(DEVICES * TILES_DEV, 1).astype(jnp.int32)


def with_ends(drawn, own_key, least, largest):
    longest = drawn.shape.index(max(drawn.shape))
    spots = []
    for shift in (0, 1):
        where = [jax.random.randint(jax.random.fold_in(own_key, axis), (), 0, length) for axis, length in enumerate(drawn.shape)]
        where[longest] = (where[longest] + shift) % drawn.shape[longest]
        spots.append(tuple(where))
    return drawn.at[spots[0]].set(least).at[spots[1]].set(largest)


def block_scale(rng, dims, cuts, least, high):
    def one(dim, parts):
        draws = jax.random.uniform(jax.random.fold_in(jax.random.fold_in(rng, 6), dim), (parts,), jnp.float32, least / len(cuts), high / len(cuts))
        return jnp.repeat(jnp.exp(draws), dims[dim] // parts).reshape((-1,) + (1,) * (len(dims) - dim - 1))

    gain = one(*cuts[0])
    for cut in cuts[1:]:
        gain = gain * one(*cut)
    return gain


def setup_inputs(seed: int = 0) -> dict:
    seeds = jax.random.split(jax.random.key(seed), 6)
    return {
        "tiles": jnp.clip(jnp.exp(math.log(5.0) - 3.2227897 * jax.random.uniform(seeds[0], (TILES, TILE, TILE), jnp.float32) ** block_scale(seeds[0], (TILES, TILE, TILE), ((0, 128),), -0.2, 0.2)), 0.19921875, 5.0).astype(jnp.bfloat16),
        "tile_dest": draw_tile_dest(jax.random.fold_in(seeds[5], 71), 0),
        "tile_slot": with_ends(jax.random.randint(seeds[2], (TILES,), 0, VIEWS * CZ), jax.random.fold_in(seeds[2], 1), 0, (VIEWS * CZ) - 1).astype(jnp.int32),
        "psf": jnp.clip(jnp.exp(jax.random.uniform(seeds[3], (VIEWS, 3, TAPS), jnp.float32, math.log(0.05), math.log(1.0))), 0.05, 1.0),
        "estimate": jnp.clip(jnp.exp(math.log(2.0) - 1.3862944 * jax.random.uniform(seeds[4], (CZ, NY, NX), jnp.float32) ** block_scale(seeds[4], (CZ, NY, NX), ((1, 8), (2, 16)), -0.2, 0.2)), 0.5, 2.0),
    }


damping = 0.05


def to_bf16(values):
    held = lax.optimization_barrier(values.astype(jnp.bfloat16))
    return held.astype(jnp.float32)


def conv_axis(volume, taps, axis):
    moved = jnp.moveaxis(volume, axis, -1)
    moved_shape = moved.shape
    rows_flat = moved.reshape(-1, 1, moved_shape[-1])
    filtered = lax.conv_general_dilated(rows_flat, taps.reshape(1, 1, -1), (1,), [(HALF, HALF)], precision=lax.Precision.HIGHEST)
    return jnp.moveaxis(filtered.reshape(moved_shape), -1, axis)


def observe(tiles_flat, target, tile_slot, view_index):
    bricks = N_GY * N_GX
    segment_ids = jnp.where(tile_slot // CZ == view_index, (tile_slot % CZ) * bricks + target, CZ * bricks).astype(jnp.int32)
    observed = jax.ops.segment_sum(tiles_flat, segment_ids, CZ * bricks + 1)[:-1]
    counted = jax.ops.segment_sum(jnp.ones(segment_ids.shape, jnp.float32), segment_ids, CZ * bricks + 1)[:-1]
    observed = observed.reshape(CZ, N_GY, N_GX, TILE, TILE).transpose(0, 1, 3, 2, 4).reshape(CZ, NY, NX)
    return observed, counted.reshape(CZ, N_GY, N_GX)


def reference(tiles, tile_dest, tile_slot, psf, estimate):
    kernel = (psf / jnp.sum(psf, axis=2, keepdims=True)).astype(jnp.bfloat16).astype(jnp.float32)
    flipped = kernel[:, :, ::-1]
    target = tile_dest[:, 0]
    tiles_flat = tiles.astype(jnp.float32).reshape(-1, TILE * TILE)
    for repeat_index in range(ITERS):
        rounded = to_bf16(estimate)
        total = jnp.zeros(estimate.shape, jnp.float32)
        for view_index in range(VIEWS):
            along_x = to_bf16(conv_axis(rounded, kernel[view_index, 2], 2))
            along_y = to_bf16(conv_axis(along_x, kernel[view_index, 1], 1))
            blur = conv_axis(along_y, kernel[view_index, 0], 0)
            observed, counted = observe(tiles_flat, target, tile_slot, view_index)
            scaled = blur.reshape(CZ, N_GY, TILE, N_GX, TILE) * counted[:, :, None, :, None]
            ratio = to_bf16((observed + damping) / (scaled.reshape(CZ, NY, NX) + damping))
            back_z = to_bf16(conv_axis(ratio, flipped[view_index, 0], 0))
            back_y = to_bf16(conv_axis(back_z, flipped[view_index, 1], 1))
            total = total + conv_axis(back_y, flipped[view_index, 2], 2)
        estimate = estimate * total / VIEWS
    return estimate
```

```python
import jax
import jax.numpy as jnp
from jax import lax
from jax.experimental import pallas as pl
from jax.experimental.pallas import tpu as pltpu
from jax.sharding import PartitionSpec as P

ITERS = 2
DAMPING = 0.05
VIEWS = 6
TAPS = 31
REACH = 15
CZ = 32
SIDE = 128
RIM = 16
EXT = SIDE + 2 * RIM
GROUPS = SIDE // RIM
ZPER = CZ // GROUPS
SLOTS = 2
HALF_TILE = 8
UX, UY, UZ, UB, UE = 2, 16, 8, 16, 4
VMEM_LIMIT = 56 * 1024 * 1024


def shift(values, axis, step):
    count = lax.axis_size(axis)
    pairs = [(i, i + step) for i in range(count) if 0 <= i + step < count]
    return lax.ppermute(values, axis, pairs)


def lanes(shape):
    return lax.broadcasted_iota(jnp.int32, shape, len(shape) - 1)


def pack_body(dest_ref, tiles_ref, out_ref, seen_ref, sem):
    count = tiles_ref.shape[0]

    @pl.loop(0, out_ref.shape[0] // SLOTS)
    def _(i):
        seen_ref[i] = 0

    @pl.loop(0, count)
    def _(i):
        target = dest_ref[i]
        rank = seen_ref[target]
        seen_ref[target] = rank + 1
        pltpu.make_async_copy(
            tiles_ref.at[i], out_ref.at[target * SLOTS + rank], sem
        ).start()

    pltpu.make_async_copy(tiles_ref, out_ref.at[pl.ds(0, count)], sem).wait()


def pack(tile_dest, tiles, devices):
    return pl.pallas_call(
        pack_body,
        out_shape=jax.ShapeDtypeStruct((devices * SLOTS,) + tiles.shape[1:], tiles.dtype),
        in_specs=[
            pl.BlockSpec(memory_space=pltpu.SMEM),
            pl.BlockSpec(memory_space=pltpu.VMEM),
        ],
        out_specs=pl.BlockSpec(memory_space=pl.ANY),
        scratch_shapes=[pltpu.SMEM((devices,), jnp.int32), pltpu.SemaphoreType.DMA(())],
        compiler_params=pltpu.CompilerParams(vmem_limit_bytes=VMEM_LIMIT),
        name="pack",
    )(tile_dest, tiles)


def unpack_body(start_ref, order_ref, got_ref, out_ref):
    base = pl.program_id(0) * CZ

    @pl.loop(0, CZ)
    def _(z):
        begin = start_ref[base + z]
        end = start_ref[base + z + 1]

        @pl.when(end == begin)
        def _():
            out_ref[0, z] = jnp.zeros((SIDE, SIDE), jnp.bfloat16)

        @pl.when(end == begin + 1)
        def _():
            out_ref[0, z] = got_ref[order_ref[begin]]

        @pl.when(end > begin + 1)
        def _():
            total = lax.fori_loop(
                begin,
                end,
                lambda j, acc: acc + got_ref[order_ref[j]].astype(jnp.float32),
                jnp.zeros((SIDE, SIDE), jnp.float32),
            )
            out_ref[0, z] = total.astype(jnp.bfloat16)


def unpack(starts, order, got):
    return pl.pallas_call(
        unpack_body,
        out_shape=jax.ShapeDtypeStruct((VIEWS, CZ) + got.shape[1:], jnp.bfloat16),
        grid_spec=pltpu.PrefetchScalarGridSpec(
            num_scalar_prefetch=2,
            grid=(VIEWS,),
            in_specs=[
                pl.BlockSpec(got.shape, lambda v, s, o: (0, 0, 0), pipeline_mode=pl.Buffered(1))
            ],
            out_specs=pl.BlockSpec((1, CZ) + got.shape[1:], lambda v, s, o: (v, 0, 0, 0)),
        ),
        compiler_params=pltpu.CompilerParams(vmem_limit_bytes=VMEM_LIMIT),
        name="unpack",
    )(starts, order, got)


def side_by_side(pair):
    return jnp.concatenate([pair[:, :HALF_TILE], pair[:, HALF_TILE:]], axis=2).reshape(
        -1, 2 * SIDE
    )


def interleave(wide):
    wide = wide.reshape(-1, HALF_TILE, 2 * SIDE)
    return jnp.concatenate([wide[:, :, :SIDE], wide[:, :, SIDE:]], axis=1)


def step_body(
    est_ref,
    top_ref,
    bot_ref,
    left_ref,
    right_ref,
    obs_ref,
    count_ref,
    wx_ref,
    wy_ref,
    wz_ref,
    bx_ref,
    by_ref,
    bz_ref,
    mid_ref,
    goleft_ref,
    goright_ref,
    wide_ref,
    ax_ref,
    ay_ref,
    rz_ref,
    ry_ref,
):
    v = pl.program_id(0)

    @pl.when(v == 0)
    def _():
        @pl.loop(0, GROUPS, unroll=UX)
        def _(g):
            z0 = g * ZPER
            wide_ref[g % UX, :, RIM : RIM + SIDE, 0:SIDE] = est_ref[pl.ds(z0, ZPER)].astype(
                jnp.bfloat16
            )
            wide_ref[g % UX, :, 0:RIM, 0:SIDE] = top_ref[pl.ds(z0, ZPER)]
            wide_ref[g % UX, :, RIM + SIDE : EXT, 0:SIDE] = bot_ref[pl.ds(z0, ZPER)]
            for q in range(ZPER):
                lane = lanes((EXT, SIDE))
                lo = pltpu.roll(left_ref[q].astype(jnp.float32), (SIDE - RIM * g) % SIDE, 1)
                hi = pltpu.roll(right_ref[q].astype(jnp.float32), (SIDE + RIM - RIM * g) % SIDE, 1)
                both = jnp.where(lane < RIM, lo, jnp.where(lane < 2 * RIM, hi, 0.0))
                wide_ref[g % UX, q, :, SIDE : 2 * SIDE] = both.astype(jnp.bfloat16)
            for q in range(ZPER):
                got = jnp.dot(
                    wide_ref[g % UX, q], wx_ref[...], preferred_element_type=jnp.float32
                ).astype(jnp.bfloat16)
                for w in range(VIEWS):
                    ax_ref[w, z0 + q] = got[:, w * SIDE : (w + 1) * SIDE]

    @pl.loop(0, CZ // 2, unroll=UY)
    def _(i):
        pair = jnp.concatenate([ax_ref[v, 2 * i], ax_ref[v, 2 * i + 1]], axis=1)
        got = jnp.dot(wy_ref[0], pair, preferred_element_type=jnp.float32)
        ay_ref[:, i] = interleave(got).astype(jnp.bfloat16)

    @pl.loop(0, SIDE // RIM, unroll=UZ)
    def _(i):
        rows = pl.ds(pl.multiple_of(i * RIM, RIM), RIM)
        one = ay_ref[2 * i].reshape(CZ * HALF_TILE, SIDE)
        two = ay_ref[2 * i + 1].reshape(CZ * HALF_TILE, SIDE)
        blur = jnp.dot(
            wz_ref[0], jnp.concatenate([one, two], axis=1), preferred_element_type=jnp.float32
        )
        seen = side_by_side(obs_ref[0, :, rows, :].astype(jnp.float32))
        times = jnp.concatenate([count_ref[0], count_ref[0]], axis=1)
        ratio = ((seen + DAMPING) / (times * blur + DAMPING)).astype(jnp.bfloat16)
        back = jnp.dot(bz_ref[0], ratio, preferred_element_type=jnp.float32)
        rz_ref[:, rows, :] = interleave(back).astype(jnp.bfloat16)

    at = pl.ds(pl.multiple_of(v * SIDE, SIDE), SIDE)

    @pl.loop(0, CZ // 2, unroll=UB)
    def _(i):
        pair = jnp.concatenate([rz_ref[2 * i], rz_ref[2 * i + 1]], axis=1)
        got = jnp.dot(by_ref[0], pair, preferred_element_type=jnp.float32).astype(jnp.bfloat16)
        ry_ref[2 * i, :, at] = got[:, :SIDE]
        ry_ref[2 * i + 1, :, at] = got[:, SIDE:]

    @pl.when(v == VIEWS - 1)
    def _():
        for q in range(ZPER):
            goleft_ref[q] = jnp.zeros((EXT, SIDE), jnp.float32)
            goright_ref[q] = jnp.zeros((EXT, SIDE), jnp.float32)

        @pl.loop(0, GROUPS, unroll=UE)
        def _(g):
            for q in range(ZPER):
                z = g * ZPER + q
                got = jnp.dot(ry_ref[z], bx_ref[...], preferred_element_type=jnp.float32)
                mid_ref[z] = got[:, :SIDE]
                strip = got[:, SIDE:]
                mine = lanes((EXT, SIDE)) // RIM == g
                goleft_ref[q] += jnp.where(mine, pltpu.roll(strip, RIM * g, 1), 0.0)
                goright_ref[q] += jnp.where(
                    mine, pltpu.roll(strip, (SIDE + RIM * g - RIM) % SIDE, 1), 0.0
                )


def whole(*shape):
    return pl.BlockSpec(shape, lambda v: (0,) * len(shape))


def per_view(*shape):
    return pl.BlockSpec((1,) + shape, lambda v: (v,) + (0,) * len(shape))


def iterate(counted, est, top, bot, left, right, observed, weights):
    wx, wy, wz, bx, by, bz = weights
    strip = jax.ShapeDtypeStruct((ZPER, EXT, SIDE), jnp.float32)
    return pl.pallas_call(
        step_body,
        out_shape=(jax.ShapeDtypeStruct((CZ, EXT, SIDE), jnp.float32), strip, strip),
        grid_spec=pltpu.PrefetchScalarGridSpec(
            num_scalar_prefetch=0,
            grid=(VIEWS,),
            in_specs=[
                whole(CZ, SIDE, SIDE),
                whole(CZ, RIM, SIDE),
                whole(CZ, RIM, SIDE),
                whole(ZPER, EXT, SIDE),
                whole(ZPER, EXT, SIDE),
                per_view(CZ, SIDE, SIDE),
                per_view(CZ * HALF_TILE, SIDE),
                whole(2 * SIDE, VIEWS * SIDE),
                per_view(SIDE, EXT),
                per_view(CZ * HALF_TILE, CZ * HALF_TILE),
                whole(VIEWS * SIDE, 2 * SIDE),
                per_view(EXT, SIDE),
                per_view(CZ * HALF_TILE, CZ * HALF_TILE),
            ],
            out_specs=(
                whole(CZ, EXT, SIDE),
                whole(ZPER, EXT, SIDE),
                whole(ZPER, EXT, SIDE),
            ),
            scratch_shapes=[
                pltpu.VMEM((UX, ZPER, EXT, 2 * SIDE), jnp.bfloat16),
                pltpu.VMEM((VIEWS, CZ, EXT, SIDE), jnp.bfloat16),
                pltpu.VMEM((SIDE // HALF_TILE, CZ // 2, RIM, SIDE), jnp.bfloat16),
                pltpu.VMEM((CZ, SIDE, SIDE), jnp.bfloat16),
                pltpu.VMEM((CZ, EXT, VIEWS * SIDE), jnp.bfloat16),
            ],
        ),
        compiler_params=pltpu.CompilerParams(vmem_limit_bytes=VMEM_LIMIT),
        name="iterate",
    )(est, top, bot, left, right, observed, counted, wx, wy, wz, bx, by, bz)


def join_x_body(mid_ref, left_ref, right_ref, up_ref, core_ref, down_ref):
    @pl.loop(0, GROUPS)
    def _(g):
        for q in range(ZPER):
            z = g * ZPER + q
            lane = lanes((EXT, SIDE))
            low = pltpu.roll(left_ref[q], (SIDE - RIM * g) % SIDE, 1)
            high = pltpu.roll(right_ref[q], (2 * SIDE - RIM - RIM * g) % SIDE, 1)
            got = mid_ref[z] + jnp.where(
                lane < RIM, low, jnp.where(lane >= SIDE - RIM, high, 0.0)
            )
            up_ref[z] = got[:RIM]
            core_ref[z] = got[RIM : RIM + SIDE]
            down_ref[z] = got[RIM + SIDE :]


def join_x(mid, from_left, from_right):
    rows = jax.ShapeDtypeStruct((CZ, RIM, SIDE), jnp.float32)
    return pl.pallas_call(
        join_x_body,
        out_shape=(rows, jax.ShapeDtypeStruct((CZ, SIDE, SIDE), jnp.float32), rows),
        compiler_params=pltpu.CompilerParams(vmem_limit_bytes=VMEM_LIMIT),
        name="join_x",
    )(mid, from_left, from_right)


def join_y_body(est_ref, core_ref, up_ref, down_ref, out_ref):
    @pl.loop(0, CZ)
    def _(z):
        head = core_ref[z, :RIM] + up_ref[z]
        tail = core_ref[z, SIDE - RIM :] + down_ref[z]
        out_ref[z, :RIM] = est_ref[z, :RIM] * head / VIEWS
        out_ref[z, RIM : SIDE - RIM] = (
            est_ref[z, RIM : SIDE - RIM] * core_ref[z, RIM : SIDE - RIM] / VIEWS
        )
        out_ref[z, SIDE - RIM :] = est_ref[z, SIDE - RIM :] * tail / VIEWS


def join_y(est, core, from_up, from_down):
    return pl.pallas_call(
        join_y_body,
        out_shape=jax.ShapeDtypeStruct(est.shape, jnp.float32),
        compiler_params=pltpu.CompilerParams(vmem_limit_bytes=VMEM_LIMIT),
        name="join_y",
    )(est, core, from_up, from_down)


def edges_body(est_ref, top_ref, bot_ref, left_ref, right_ref):
    for q in range(ZPER):
        left_ref[q] = jnp.zeros((EXT, SIDE), jnp.bfloat16)
        right_ref[q] = jnp.zeros((EXT, SIDE), jnp.bfloat16)

    @pl.loop(0, GROUPS)
    def _(g):
        for q in range(ZPER):
            z = g * ZPER + q
            plane = jnp.concatenate(
                [top_ref[z].astype(jnp.float32), est_ref[z], bot_ref[z].astype(jnp.float32)],
                axis=0,
            )
            mine = lanes((EXT, SIDE)) // RIM == g
            low = pltpu.roll(plane, RIM * g, 1)
            high = pltpu.roll(plane, (RIM * g + RIM) % SIDE, 1)
            left_ref[q] += jnp.where(mine, low, 0.0).astype(jnp.bfloat16)
            right_ref[q] += jnp.where(mine, high, 0.0).astype(jnp.bfloat16)


def edges(est, top, bot):
    strip = jax.ShapeDtypeStruct((ZPER, EXT, SIDE), jnp.bfloat16)
    return pl.pallas_call(
        edges_body,
        out_shape=(strip, strip),
        compiler_params=pltpu.CompilerParams(vmem_limit_bytes=VMEM_LIMIT),
        name="edges",
    )(est, top, bot)


def surround(est):
    top = shift(est[:, SIDE - RIM :].astype(jnp.bfloat16), "gy", 1)
    bot = shift(est[:, :RIM].astype(jnp.bfloat16), "gy", -1)
    low, high = edges(est, top, bot)
    return top, bot, shift(high, "gx", 1), shift(low, "gx", -1)


def pick(taps, offset):
    hot = (offset[:, :, None] == jnp.arange(TAPS)[None, None, :]).astype(jnp.bfloat16)
    return jnp.einsum("rct,vt->vrc", hot, taps, preferred_element_type=jnp.float32).astype(
        jnp.bfloat16
    )


def weights_of(psf):
    kernel = (psf / jnp.sum(psf, axis=2, keepdims=True)).astype(jnp.bfloat16)
    core = jnp.arange(SIDE)
    rim = jnp.arange(RIM)
    far = jnp.full((SIDE - 2 * RIM,), 4 * SIDE)
    where_x = jnp.concatenate([core, rim - RIM, SIDE + rim, far])
    wx = pick(kernel[:, 2], where_x[:, None] - core[None, :] + REACH)
    wx = jnp.transpose(wx, (1, 0, 2)).reshape(2 * SIDE, VIEWS * SIDE)
    bx = pick(kernel[:, 2], where_x[None, :] - core[:, None] + REACH).reshape(
        VIEWS * SIDE, 2 * SIDE
    )
    where_y = jnp.arange(EXT) - RIM
    wy = pick(kernel[:, 1], where_y[None, :] - core[:, None] + REACH)
    by = pick(kernel[:, 1], where_y[:, None] - core[None, :] + REACH)
    row = jnp.arange(CZ * HALF_TILE)
    same = row[:, None] % HALF_TILE == row[None, :] % HALF_TILE
    gap = row[None, :] // HALF_TILE - row[:, None] // HALF_TILE
    wz = pick(kernel[:, 0], jnp.where(same, gap + REACH, -1))
    bz = pick(kernel[:, 0], jnp.where(same, REACH - gap, -1))
    return wx, wy, wz, bx, by, bz


def local(tiles, tile_dest, tile_slot, psf, estimate):
    axes = ("gy", "gx")
    devices = lax.axis_size("gy") * lax.axis_size("gx")
    dest = tile_dest[:, 0]
    count = dest.shape[0]
    at = jnp.arange(count)
    hit = dest[None, :] == jnp.arange(devices)[:, None]
    first = jnp.min(jnp.where(hit, at[None, :] * 256 + tile_slot[None, :], count * 256), axis=1)
    last = jnp.max(jnp.where(hit, at[None, :] * 256 + tile_slot[None, :], -1), axis=1)
    labels = jnp.stack(
        [
            jnp.where(first < count * 256, first % 256, 255),
            jnp.where(last > first, last % 256, 255),
        ],
        axis=1,
    )
    labels = lax.all_to_all(labels, axes, split_axis=0, concat_axis=0, tiled=True).reshape(-1)
    got = lax.all_to_all(
        pack(dest, tiles, devices), axes, split_axis=0, concat_axis=0, tiled=True
    )
    kinds = jnp.arange(VIEWS * CZ + 1)
    starts = jnp.sum((labels[None, :] < kinds[:, None]).astype(jnp.int32), axis=1)
    slots = jnp.arange(labels.shape[0])
    keys = labels * 512 + slots
    place = jnp.sum((keys[None, :] < keys[:, None]).astype(jnp.int32), axis=1)
    order = jnp.sum(jnp.where(place[None, :] == slots[:, None], slots[None, :], 0), axis=1)
    counted = (starts[1:] - starts[:-1]).astype(jnp.float32).reshape(VIEWS, CZ, 1, 1)
    counted = jnp.broadcast_to(counted, (VIEWS, CZ, HALF_TILE, SIDE)).reshape(VIEWS, -1, SIDE)
    weights = weights_of(psf)
    around = surround(estimate)
    observed = unpack(starts, order, got)
    for repeat_index in range(ITERS):
        mid, goleft, goright = iterate(counted, estimate, *around, observed, weights)
        up, core, down = join_x(mid, shift(goright, "gx", 1), shift(goleft, "gx", -1))
        estimate = join_y(estimate, core, shift(down, "gy", 1), shift(up, "gy", -1))
        if repeat_index + 1 < ITERS:
            around = surround(estimate)
    return estimate


def solution(mesh):
    placed = (
        P(("gy", "gx"), None, None),
        P(("gy", "gx"), None),
        P(("gy", "gx")),
        P(),
        P(None, "gy", "gx"),
    )
    return jax.shard_map(
        local, mesh=mesh, in_specs=placed, out_specs=P(None, "gy", "gx"), check_vma=False
    )
```

```python
import jax
import jax.numpy as jnp
from jax import lax
from jax.experimental import pallas as pl
from jax.experimental.pallas import tpu as pltpu
from jax.sharding import PartitionSpec as P

ITERS = 2
DAMPING = 0.05
VIEWS = 6
TAPS = 31
REACH = 15
CZ = 32
SIDE = 128
RIM = 16
EXT = SIDE + 2 * RIM
GROUPS = SIDE // RIM
ZPER = CZ // GROUPS
SLOTS = 2
HALF_TILE = 8
UX, UY, UZ, UB, UE = 2, 16, 8, 16, 2
VMEM_LIMIT = 56 * 1024 * 1024


def shift(values, axis, step):
    count = lax.axis_size(axis)
    pairs = [(i, i + step) for i in range(count) if 0 <= i + step < count]
    return lax.ppermute(values, axis, pairs)


def lanes(shape):
    return lax.broadcasted_iota(jnp.int32, shape, len(shape) - 1)


def pack_body(dest_ref, tiles_ref, labels_ref, out_ref, seen_ref, tile_sem, label_sem):
    count = tiles_ref.shape[0]
    devices = out_ref.shape[0]
    named = pltpu.make_async_copy(
        labels_ref, out_ref.at[:, pl.ds(SLOTS * SIDE, HALF_TILE)], label_sem
    )
    named.start()

    @pl.loop(0, devices)
    def _(i):
        seen_ref[i] = 0

    @pl.loop(0, count)
    def _(i):
        target = dest_ref[i]
        rank = seen_ref[target]
        seen_ref[target] = rank + 1
        pltpu.make_async_copy(
            tiles_ref.at[i], out_ref.at[target, pl.ds(rank * SIDE, SIDE)], tile_sem
        ).start()

    every = out_ref.at[pl.ds(0, count // SLOTS), pl.ds(0, SLOTS * SIDE)]
    pltpu.make_async_copy(every, every, tile_sem).wait()
    named.wait()


def pack(tile_dest, tiles, labels):
    devices = labels.shape[0]
    return pl.pallas_call(
        pack_body,
        out_shape=jax.ShapeDtypeStruct((devices, SLOTS * SIDE + HALF_TILE, SIDE), tiles.dtype),
        in_specs=[
            pl.BlockSpec(memory_space=pltpu.SMEM),
            pl.BlockSpec(memory_space=pltpu.VMEM),
            pl.BlockSpec(memory_space=pltpu.VMEM),
        ],
        out_specs=pl.BlockSpec(memory_space=pl.ANY),
        scratch_shapes=[
            pltpu.SMEM((devices,), jnp.int32),
            pltpu.SemaphoreType.DMA(()),
            pltpu.SemaphoreType.DMA(()),
        ],
        compiler_params=pltpu.CompilerParams(vmem_limit_bytes=VMEM_LIMIT),
        name="pack",
    )(tile_dest, tiles, labels)


def side_by_side(pair):
    return jnp.concatenate([pair[:, :HALF_TILE], pair[:, HALF_TILE:]], axis=2).reshape(
        -1, 2 * SIDE
    )


def interleave(wide):
    wide = wide.reshape(-1, HALF_TILE, 2 * SIDE)
    return jnp.concatenate([wide[:, :, :SIDE], wide[:, :, SIDE:]], axis=1)


def filter_x(est_ref, top_ref, bot_ref, left_ref, right_ref, wx_ref, wide_ref, ax_ref):
    @pl.loop(0, GROUPS, unroll=UX)
    def _(g):
        z0 = g * ZPER
        slot = g % UX
        wide_ref[slot, :, RIM : RIM + SIDE, 0:SIDE] = est_ref[pl.ds(z0, ZPER)].astype(
            jnp.bfloat16
        )
        wide_ref[slot, :, 0:RIM, 0:SIDE] = top_ref[pl.ds(z0, ZPER)]
        wide_ref[slot, :, RIM + SIDE : EXT, 0:SIDE] = bot_ref[pl.ds(z0, ZPER)]
        for q in range(ZPER):
            lane = lanes((EXT, SIDE))
            lo = pltpu.roll(left_ref[q].astype(jnp.float32), (SIDE - RIM * g) % SIDE, 1)
            hi = pltpu.roll(right_ref[q].astype(jnp.float32), (SIDE + RIM - RIM * g) % SIDE, 1)
            both = jnp.where(lane < RIM, lo, jnp.where(lane < 2 * RIM, hi, 0.0))
            wide_ref[slot, q, :, SIDE : 2 * SIDE] = both.astype(jnp.bfloat16)
        for q in range(ZPER):
            got = jnp.dot(
                wide_ref[slot, q], wx_ref[...], preferred_element_type=jnp.float32
            ).astype(jnp.bfloat16)
            for w in range(VIEWS):
                ax_ref[w, z0 + q] = got[:, w * SIDE : (w + 1) * SIDE]


def filter_y(v, wy_ref, ax_ref, ay_ref):
    @pl.loop(0, CZ // 2, unroll=UY)
    def _(i):
        pair = jnp.concatenate([ax_ref[v, 2 * i], ax_ref[v, 2 * i + 1]], axis=1)
        got = jnp.dot(wy_ref[0], pair, preferred_element_type=jnp.float32)
        ay_ref[:, i] = interleave(got).astype(jnp.bfloat16)


def filter_z(i, wz_ref, ay_ref):
    one = ay_ref[2 * i].reshape(CZ * HALF_TILE, SIDE)
    two = ay_ref[2 * i + 1].reshape(CZ * HALF_TILE, SIDE)
    return jnp.dot(
        wz_ref[0], jnp.concatenate([one, two], axis=1), preferred_element_type=jnp.float32
    )


def compare(i, blur, seen, count_ref, bz_ref, rz_ref):
    rows = pl.ds(pl.multiple_of(i * RIM, RIM), RIM)
    seen = side_by_side(seen.astype(jnp.float32))
    times = jnp.concatenate([count_ref[0], count_ref[0]], axis=1)
    ratio = ((seen + DAMPING) / (times * blur + DAMPING)).astype(jnp.bfloat16)
    back = jnp.dot(bz_ref[0], ratio, preferred_element_type=jnp.float32)
    rz_ref[:, rows, :] = interleave(back).astype(jnp.bfloat16)


def spread_y(v, by_ref, rz_ref, ry_ref):
    at = pl.ds(pl.multiple_of(v * SIDE, SIDE), SIDE)

    @pl.loop(0, CZ // 2, unroll=UB)
    def _(i):
        pair = jnp.concatenate([rz_ref[2 * i], rz_ref[2 * i + 1]], axis=1)
        got = jnp.dot(by_ref[0], pair, preferred_element_type=jnp.float32).astype(jnp.bfloat16)
        ry_ref[2 * i, :, at] = got[:, :SIDE]
        ry_ref[2 * i + 1, :, at] = got[:, SIDE:]


def spread_x(bx_ref, ry_ref, mid_ref, up_ref, down_ref, goleft_ref, goright_ref):
    @pl.loop(0, ZPER, unroll=UE)
    def _(q):
        goleft = jnp.zeros((EXT, SIDE), jnp.float32)
        goright = jnp.zeros((EXT, SIDE), jnp.float32)
        for g in range(GROUPS):
            z = g * ZPER + q
            got = jnp.dot(ry_ref[z], bx_ref[...], preferred_element_type=jnp.float32)
            up_ref[z] = got[:RIM, :SIDE]
            mid_ref[z] = got[RIM : RIM + SIDE, :SIDE]
            down_ref[z] = got[RIM + SIDE :, :SIDE]
            strip = got[:, SIDE:]
            mine = lanes((EXT, SIDE)) // RIM == g
            goleft = jnp.where(mine, pltpu.roll(strip, RIM * g, 1), goleft)
            goright = jnp.where(mine, pltpu.roll(strip, (SIDE + RIM * g - RIM) % SIDE, 1), goright)
        goleft_ref[q] = goleft
        goright_ref[q] = goright


def forward_body(
    est_ref, top_ref, bot_ref, left_ref, right_ref, wx_ref, wy_ref, wz_ref,
    blur_ref, wide_ref, ax_ref, ay_ref,
):
    v = pl.program_id(0)

    @pl.when(v == 0)
    def _():
        filter_x(est_ref, top_ref, bot_ref, left_ref, right_ref, wx_ref, wide_ref, ax_ref)

    filter_y(v, wy_ref, ax_ref, ay_ref)

    @pl.loop(0, SIDE // RIM, unroll=UZ)
    def _(i):
        blur_ref[0, i] = filter_z(i, wz_ref, ay_ref)


def backward_body(
    label_ref, got_ref, blur_ref, bx_ref, by_ref, bz_ref,
    mid_ref, up_ref, down_ref, goleft_ref, goright_ref, obs_ref, count_ref,
    rz_ref, ry_ref, head_ref, next_ref, times_ref,
):
    v = pl.program_id(0)

    @pl.when(v == 0)
    def _():
        @pl.loop(0, VIEWS * CZ)
        def _(i):
            head_ref[i] = -1
            times_ref[i] = 0

        @pl.loop(0, label_ref.shape[0])
        def _(i):
            label = label_ref[i]

            @pl.when(label >= 0)
            def _():
                next_ref[i] = head_ref[label]
                head_ref[label] = i
                times_ref[label] = times_ref[label] + 1

    def tile(i):
        return got_ref[i // SLOTS, pl.ds(pl.multiple_of(i % SLOTS * SIDE, SIDE), SIDE)]

    @pl.loop(0, CZ)
    def _(z):
        first = head_ref[v * CZ + z]
        times = times_ref[v * CZ + z]
        count_ref[0, pl.ds(pl.multiple_of(z * HALF_TILE, HALF_TILE), HALF_TILE)] = jnp.full(
            (HALF_TILE, SIDE), times.astype(jnp.float32)
        )

        @pl.when(times == 0)
        def _():
            obs_ref[0, z] = jnp.zeros((SIDE, SIDE), jnp.bfloat16)

        @pl.when(times == 1)
        def _():
            obs_ref[0, z] = tile(first)

        @pl.when(times > 1)
        def _():
            def add(_, carry):
                at, total = carry
                return next_ref[at], total + tile(at).astype(jnp.float32)

            total = jnp.zeros((SIDE, SIDE), jnp.float32)
            obs_ref[0, z] = lax.fori_loop(0, times, add, (first, total))[1].astype(jnp.bfloat16)

    @pl.loop(0, SIDE // RIM, unroll=UZ)
    def _(i):
        rows = pl.ds(pl.multiple_of(i * RIM, RIM), RIM)
        compare(i, blur_ref[0, i], obs_ref[0, :, rows, :], count_ref, bz_ref, rz_ref)

    spread_y(v, by_ref, rz_ref, ry_ref)

    @pl.when(v == VIEWS - 1)
    def _():
        spread_x(bx_ref, ry_ref, mid_ref, up_ref, down_ref, goleft_ref, goright_ref)


def step_body(
    est_ref, top_ref, bot_ref, left_ref, right_ref, obs_ref, count_ref,
    wx_ref, wy_ref, wz_ref, bx_ref, by_ref, bz_ref,
    mid_ref, up_ref, down_ref, goleft_ref, goright_ref,
    wide_ref, ax_ref, ay_ref, rz_ref, ry_ref,
):
    v = pl.program_id(0)

    @pl.when(v == 0)
    def _():
        filter_x(est_ref, top_ref, bot_ref, left_ref, right_ref, wx_ref, wide_ref, ax_ref)

    filter_y(v, wy_ref, ax_ref, ay_ref)

    @pl.loop(0, SIDE // RIM, unroll=UZ)
    def _(i):
        rows = pl.ds(pl.multiple_of(i * RIM, RIM), RIM)
        blur = filter_z(i, wz_ref, ay_ref)
        compare(i, blur, obs_ref[0, :, rows, :], count_ref, bz_ref, rz_ref)

    spread_y(v, by_ref, rz_ref, ry_ref)

    @pl.when(v == VIEWS - 1)
    def _():
        spread_x(bx_ref, ry_ref, mid_ref, up_ref, down_ref, goleft_ref, goright_ref)


def whole(*shape):
    return pl.BlockSpec(shape, lambda v, *_: (0,) * len(shape))


def once(*shape):
    return pl.BlockSpec(
        shape, lambda v, *_: (0,) * len(shape), pipeline_mode=pl.Buffered(1)
    )


def per_view(*shape):
    return pl.BlockSpec((1,) + shape, lambda v, *_: (v,) + (0,) * len(shape))


ROWS = (CZ, RIM, SIDE)
CORE = (CZ, SIDE, SIDE)
STRIP = (ZPER, EXT, SIDE)
Z_BAND = (CZ * HALF_TILE, CZ * HALF_TILE)
TIMES = (CZ * HALF_TILE, SIDE)
BLUR = (SIDE // RIM, CZ * HALF_TILE, 2 * SIDE)
HALO_SPECS = [whole(*ROWS), whole(*ROWS), whole(*STRIP), whole(*STRIP)]
FRONT_SPECS = [whole(2 * SIDE, VIEWS * SIDE), per_view(SIDE, EXT), per_view(*Z_BAND)]
BACK_SPECS = [whole(VIEWS * SIDE, 2 * SIDE), per_view(EXT, SIDE), per_view(*Z_BAND)]
PART_SPECS = [whole(*CORE), whole(*ROWS), whole(*ROWS), whole(*STRIP), whole(*STRIP)]
PARTS = tuple(
    jax.ShapeDtypeStruct(shape, jnp.float32) for shape in (CORE, ROWS, ROWS, STRIP, STRIP)
)
FRONT_SCRATCH = [
    pltpu.VMEM((UX, ZPER, EXT, 2 * SIDE), jnp.bfloat16),
    pltpu.VMEM((VIEWS, CZ, EXT, SIDE), jnp.bfloat16),
    pltpu.VMEM((SIDE // HALF_TILE, CZ // 2, RIM, SIDE), jnp.bfloat16),
]
BACK_SCRATCH = [
    pltpu.VMEM(CORE, jnp.bfloat16),
    pltpu.VMEM((CZ, EXT, VIEWS * SIDE), jnp.bfloat16),
]
ROOM = pltpu.CompilerParams(vmem_limit_bytes=VMEM_LIMIT)


def forward(est, halo, weights):
    return pl.pallas_call(
        forward_body,
        out_shape=jax.ShapeDtypeStruct((VIEWS,) + BLUR, jnp.float32),
        grid=(VIEWS,),
        in_specs=[whole(*CORE)] + HALO_SPECS + FRONT_SPECS,
        out_specs=per_view(*BLUR),
        scratch_shapes=FRONT_SCRATCH,
        compiler_params=ROOM,
        name="forward",
    )(est, *halo, *weights[:3])


def backward(labels, got, blur, weights):
    slots = labels.shape[0]
    return pl.pallas_call(
        backward_body,
        out_shape=PARTS
        + (
            jax.ShapeDtypeStruct((VIEWS,) + CORE, jnp.bfloat16),
            jax.ShapeDtypeStruct((VIEWS,) + TIMES, jnp.float32),
        ),
        grid_spec=pltpu.PrefetchScalarGridSpec(
            num_scalar_prefetch=1,
            grid=(VIEWS,),
            in_specs=[once(*got.shape), per_view(*BLUR)] + BACK_SPECS,
            out_specs=PART_SPECS + [per_view(*CORE), per_view(*TIMES)],
            scratch_shapes=BACK_SCRATCH
            + [
                pltpu.SMEM((VIEWS * CZ,), jnp.int32),
                pltpu.SMEM((slots,), jnp.int32),
                pltpu.SMEM((VIEWS * CZ,), jnp.int32),
            ],
        ),
        compiler_params=ROOM,
        name="backward",
    )(labels, got, blur, *weights[3:])


def iterate(counted, est, halo, observed, weights):
    return pl.pallas_call(
        step_body,
        out_shape=PARTS,
        grid=(VIEWS,),
        in_specs=[whole(*CORE)]
        + HALO_SPECS
        + [per_view(*CORE), per_view(*TIMES)]
        + FRONT_SPECS
        + BACK_SPECS,
        out_specs=PART_SPECS,
        scratch_shapes=FRONT_SCRATCH + BACK_SCRATCH,
        compiler_params=ROOM,
        name="iterate",
    )(est, *halo, observed, counted, *weights)


def beside(q, g, rows, left_ref, right_ref):
    low = pltpu.roll(left_ref[q, rows], (SIDE - RIM * g) % SIDE, 1)
    high = pltpu.roll(right_ref[q, rows], (2 * SIDE - RIM - RIM * g) % SIDE, 1)
    lane = lanes(low.shape)
    return jnp.where(lane < RIM, low, jnp.where(lane >= SIDE - RIM, high, 0.0))


def in_two(values):
    high = values.astype(jnp.bfloat16)
    return high, (values - high.astype(jnp.float32)).astype(jnp.bfloat16)


def join_x_body(first_ref, last_ref, up_ref, down_ref, left_ref, right_ref, *outs):
    @pl.loop(0, ZPER, unroll=True)
    def _(q):
        for g in range(GROUPS):
            z = g * ZPER + q
            head = up_ref[z] + beside(q, g, slice(0, RIM), left_ref, right_ref)
            tail = down_ref[z] + beside(q, g, slice(SIDE + RIM, EXT), left_ref, right_ref)
            outs[0][z], outs[1][z] = head, tail
            if len(outs) > 2:
                own = first_ref[z] + beside(q, g, slice(RIM, 2 * RIM), left_ref, right_ref)
                outs[2][z], outs[2][CZ + z] = in_two(head)
                outs[2][2 * CZ + z] = own.astype(jnp.bfloat16)
                own = last_ref[z] + beside(q, g, slice(SIDE, SIDE + RIM), left_ref, right_ref)
                outs[3][z], outs[3][CZ + z] = in_two(tail)
                outs[3][2 * CZ + z] = own.astype(jnp.bfloat16)


def join_x(mid, up, down, from_left, from_right, more):
    rows = jax.ShapeDtypeStruct(ROWS, jnp.float32)
    message = jax.ShapeDtypeStruct((3 * CZ, RIM, SIDE), jnp.bfloat16)
    out_shape = (rows, rows) + ((message, message) if more else ())
    return pl.pallas_call(
        join_x_body,
        out_shape=out_shape,
        grid=(1,),
        in_specs=[
            pl.BlockSpec(ROWS, lambda i: (0, 0, 0)),
            pl.BlockSpec(ROWS, lambda i: (0, SIDE // RIM - 1, 0)),
            whole(*ROWS),
            whole(*ROWS),
            whole(*STRIP),
            whole(*STRIP),
        ],
        out_specs=[whole(*shape.shape) for shape in out_shape],
        compiler_params=ROOM,
        name="join_x",
    )(mid, mid, up, down, from_left, from_right)


def joined(est_ref, mid_ref, left_ref, right_ref, q, g, head, tail):
    z = g * ZPER + q
    total = mid_ref[z] + beside(q, g, slice(RIM, RIM + SIDE), left_ref, right_ref)
    total = jnp.concatenate(
        [total[:RIM] + head, total[RIM : SIDE - RIM], total[SIDE - RIM :] + tail], axis=0
    )
    return est_ref[z] * total / VIEWS


def last_join_body(est_ref, mid_ref, left_ref, right_ref, above_ref, below_ref, out_ref):
    @pl.loop(0, ZPER, unroll=2)
    def _(q):
        for g in range(GROUPS):
            z = g * ZPER + q
            out_ref[z] = joined(
                est_ref, mid_ref, left_ref, right_ref, q, g, above_ref[z], below_ref[z]
            )


def last_join(est, mid, from_left, from_right, above, below):
    return pl.pallas_call(
        last_join_body,
        out_shape=jax.ShapeDtypeStruct(CORE, jnp.float32),
        compiler_params=ROOM,
        name="last_join",
    )(est, mid, from_left, from_right, above, below)


def cut(q, planes, left_ref, right_ref):
    low = jnp.zeros((EXT, SIDE), jnp.float32)
    high = jnp.zeros((EXT, SIDE), jnp.float32)
    for g, plane in enumerate(planes):
        mine = lanes((EXT, SIDE)) // RIM == g
        low = jnp.where(mine, pltpu.roll(plane, RIM * g, 1), low)
        high = jnp.where(mine, pltpu.roll(plane, (RIM * g + RIM) % SIDE, 1), high)
    left_ref[q] = low.astype(jnp.bfloat16)
    right_ref[q] = high.astype(jnp.bfloat16)


def next_join_body(
    est_ref, mid_ref, left_ref, right_ref, above_ref, below_ref,
    up_ref, down_ref, top_ref, bot_ref,
    out_ref, newtop_ref, newbot_ref, goleft_ref, goright_ref,
):
    def whole_of(ref, z):
        return ref[z].astype(jnp.float32) + ref[CZ + z].astype(jnp.float32)

    @pl.loop(0, ZPER, unroll=2)
    def _(q):
        planes = []
        for g in range(GROUPS):
            z = g * ZPER + q
            now = joined(
                est_ref, mid_ref, left_ref, right_ref, q, g,
                whole_of(above_ref, z), whole_of(below_ref, z),
            )
            out_ref[z] = now
            total = above_ref[2 * CZ + z].astype(jnp.float32) + up_ref[z]
            newtop = top_ref[z].astype(jnp.float32) * total / VIEWS
            newtop_ref[z] = newtop.astype(jnp.bfloat16)
            total = below_ref[2 * CZ + z].astype(jnp.float32) + down_ref[z]
            newbot = bot_ref[z].astype(jnp.float32) * total / VIEWS
            newbot_ref[z] = newbot.astype(jnp.bfloat16)
            planes.append(jnp.concatenate([newtop, now, newbot], axis=0))
        cut(q, planes, goleft_ref, goright_ref)


def next_join(est, mid, from_left, from_right, above, below, up, down, top, bot):
    rows = jax.ShapeDtypeStruct(ROWS, jnp.bfloat16)
    strip = jax.ShapeDtypeStruct(STRIP, jnp.bfloat16)
    return pl.pallas_call(
        next_join_body,
        out_shape=(jax.ShapeDtypeStruct(CORE, jnp.float32), rows, rows, strip, strip),
        compiler_params=ROOM,
        name="next_join",
    )(est, mid, from_left, from_right, above, below, up, down, top, bot)


def edges_body(est_ref, top_ref, bot_ref, left_ref, right_ref):
    @pl.loop(0, ZPER, unroll=2)
    def _(q):
        planes = []
        for g in range(GROUPS):
            z = g * ZPER + q
            rim = (top_ref[z].astype(jnp.float32), bot_ref[z].astype(jnp.float32))
            planes.append(jnp.concatenate([rim[0], est_ref[z], rim[1]], axis=0))
        cut(q, planes, left_ref, right_ref)


def edges(est, top, bot):
    strip = jax.ShapeDtypeStruct(STRIP, jnp.bfloat16)
    return pl.pallas_call(
        edges_body,
        out_shape=(strip, strip),
        compiler_params=ROOM,
        name="edges",
    )(est, top, bot)


def pick(taps, offset):
    hot = (offset[:, :, None] == jnp.arange(TAPS)[None, None, :]).astype(jnp.bfloat16)
    return jnp.einsum("rct,vt->vrc", hot, taps, preferred_element_type=jnp.float32).astype(
        jnp.bfloat16
    )


def weights_of(psf):
    kernel = (psf / jnp.sum(psf, axis=2, keepdims=True)).astype(jnp.bfloat16)
    core = jnp.arange(SIDE)
    rim = jnp.arange(RIM)
    far = jnp.full((SIDE - 2 * RIM,), 4 * SIDE)
    where_x = jnp.concatenate([core, rim - RIM, SIDE + rim, far])
    wx = pick(kernel[:, 2], where_x[:, None] - core[None, :] + REACH)
    wx = jnp.transpose(wx, (1, 0, 2)).reshape(2 * SIDE, VIEWS * SIDE)
    bx = pick(kernel[:, 2], where_x[None, :] - core[:, None] + REACH).reshape(
        VIEWS * SIDE, 2 * SIDE
    )
    where_y = jnp.arange(EXT) - RIM
    wy = pick(kernel[:, 1], where_y[None, :] - core[:, None] + REACH)
    by = pick(kernel[:, 1], where_y[:, None] - core[None, :] + REACH)
    row = jnp.arange(CZ * HALF_TILE)
    same = row[:, None] % HALF_TILE == row[None, :] % HALF_TILE
    gap = row[None, :] // HALF_TILE - row[:, None] // HALF_TILE
    wz = pick(kernel[:, 0], jnp.where(same, gap + REACH, -1))
    bz = pick(kernel[:, 0], jnp.where(same, REACH - gap, -1))
    return wx, wy, wz, bx, by, bz


def local(tiles, tile_dest, tile_slot, psf, estimate):
    axes = ("gy", "gx")
    devices = lax.axis_size("gy") * lax.axis_size("gx")
    top = shift(estimate[:, SIDE - RIM :].astype(jnp.bfloat16), "gy", 1)
    bot = shift(estimate[:, :RIM].astype(jnp.bfloat16), "gy", -1)
    dest = tile_dest[:, 0]
    count = dest.shape[0]
    order = (jnp.arange(count) * 256 + tile_slot)[None, :]
    hit = dest[None, :] == jnp.arange(devices)[:, None]
    first = jnp.min(jnp.where(hit, order, count * 256), axis=1)[:, None, None]
    last = jnp.max(jnp.where(hit, order, -1), axis=1)[:, None, None]
    one = jnp.where(first < count * 256, first % 256, -1)
    two = jnp.where(last > first, last % 256, -1)
    labels = jnp.where(lanes((devices, HALF_TILE, SIDE)) == 0, one, two).astype(jnp.bfloat16)
    low, high = edges(estimate, top, bot)
    left, right = shift(high, "gx", 1), shift(low, "gx", -1)
    packed = pack(dest, tiles, labels)
    packed, left, right = lax.optimization_barrier((packed, left, right))
    got = lax.all_to_all(packed, axes, split_axis=0, concat_axis=0, tiled=True)
    weights = weights_of(psf)
    blur = forward(estimate, (top, bot, left, right), weights)
    labels = got[:, SLOTS * SIDE, :SLOTS].astype(jnp.int32).reshape(-1)
    *parts, observed, counted = backward(labels, got, blur, weights)
    for repeat_index in range(ITERS):
        more = repeat_index + 1 < ITERS
        mid, up, down, goleft, goright = parts
        sides = shift(goright, "gx", 1), shift(goleft, "gx", -1)
        sent = join_x(mid, up, down, *sides, more)
        if not more:
            up, down = sent
            return last_join(
                estimate, mid, *sides, shift(down, "gy", 1), shift(up, "gy", -1)
            )
        up, down, goup, godown = sent
        estimate, top, bot, low, high = next_join(
            estimate, mid, *sides, shift(godown, "gy", 1), shift(goup, "gy", -1), up, down, top, bot
        )
        halo = top, bot, shift(high, "gx", 1), shift(low, "gx", -1)
        parts = iterate(counted, estimate, halo, observed, weights)


def solution(mesh):
    placed = (
        P(("gy", "gx"), None, None),
        P(("gy", "gx"), None),
        P(("gy", "gx")),
        P(),
        P(None, "gy", "gx"),
    )
    return jax.shard_map(
        local, mesh=mesh, in_specs=placed, out_specs=P(None, "gy", "gx"), check_vma=False
    )
```

```python
import jax
import jax.numpy as jnp
from jax import lax
from jax.experimental import pallas as pl
from jax.experimental.pallas import tpu as pltpu
from jax.sharding import PartitionSpec as P

ITERS = 2
DAMPING = 0.05
VIEWS = 6
TAPS = 31
REACH = 15
CZ = 32
SIDE = 128
RIM = 16
EXT = SIDE + 2 * RIM
GROUPS = SIDE // RIM
ZPER = CZ // GROUPS
SLOTS = 2
HALF_TILE = 8
UX, UY, UZ, UB, UE = 2, 16, 8, 16, 2
def room(mebibytes):
    return pltpu.CompilerParams(vmem_limit_bytes=mebibytes << 20)


def shift(values, axis, step):
    count = lax.axis_size(axis)
    pairs = [(i, i + step) for i in range(count) if 0 <= i + step < count]
    return lax.ppermute(values, axis, pairs)


def lanes(shape):
    return lax.broadcasted_iota(jnp.int32, shape, len(shape) - 1)


def pack_body(dest_ref, tiles_ref, labels_ref, out_ref, seen_ref, tile_sem, label_sem):
    count = tiles_ref.shape[0]
    devices = out_ref.shape[0]
    named = pltpu.make_async_copy(
        labels_ref, out_ref.at[:, pl.ds(SLOTS * SIDE, HALF_TILE)], label_sem
    )
    named.start()

    @pl.loop(0, devices)
    def _(i):
        seen_ref[i] = 0

    @pl.loop(0, count)
    def _(i):
        target = dest_ref[i]
        rank = seen_ref[target]
        seen_ref[target] = rank + 1
        pltpu.make_async_copy(
            tiles_ref.at[i], out_ref.at[target, pl.ds(rank * SIDE, SIDE)], tile_sem
        ).start()

    every = out_ref.at[pl.ds(0, count // SLOTS), pl.ds(0, SLOTS * SIDE)]
    pltpu.make_async_copy(every, every, tile_sem).wait()
    named.wait()


def pack(tile_dest, tiles, labels):
    devices = labels.shape[0]
    return pl.pallas_call(
        pack_body,
        out_shape=jax.ShapeDtypeStruct((devices, SLOTS * SIDE + HALF_TILE, SIDE), tiles.dtype),
        in_specs=[
            pl.BlockSpec(memory_space=pltpu.SMEM),
            pl.BlockSpec(memory_space=pltpu.VMEM),
            pl.BlockSpec(memory_space=pltpu.VMEM),
        ],
        out_specs=pl.BlockSpec(memory_space=pltpu.HBM),
        scratch_shapes=[
            pltpu.SMEM((devices,), jnp.int32),
            pltpu.SemaphoreType.DMA(()),
            pltpu.SemaphoreType.DMA(()),
        ],
        compiler_params=room(56),
        name="pack",
    )(tile_dest, tiles, labels)


def side_by_side(pair):
    return jnp.concatenate([pair[:, :HALF_TILE], pair[:, HALF_TILE:]], axis=2).reshape(
        -1, 2 * SIDE
    )


def interleave(wide):
    wide = wide.reshape(-1, HALF_TILE, 2 * SIDE)
    return jnp.concatenate([wide[:, :, :SIDE], wide[:, :, SIDE:]], axis=1)


def filter_x(est_ref, top_ref, bot_ref, left_ref, right_ref, wx_ref, wide_ref, ax_ref):
    @pl.loop(0, GROUPS, unroll=UX)
    def _(g):
        z0 = g * ZPER
        slot = g % UX
        wide_ref[slot, :, RIM : RIM + SIDE, 0:SIDE] = est_ref[pl.ds(z0, ZPER)].astype(
            jnp.bfloat16
        )
        wide_ref[slot, :, 0:RIM, 0:SIDE] = top_ref[pl.ds(z0, ZPER)]
        wide_ref[slot, :, RIM + SIDE : EXT, 0:SIDE] = bot_ref[pl.ds(z0, ZPER)]
        for q in range(ZPER):
            lane = lanes((EXT, SIDE))
            lo = pltpu.roll(left_ref[q].astype(jnp.float32), (SIDE - RIM * g) % SIDE, 1)
            hi = pltpu.roll(right_ref[q].astype(jnp.float32), (SIDE + RIM - RIM * g) % SIDE, 1)
            both = jnp.where(lane < RIM, lo, jnp.where(lane < 2 * RIM, hi, 0.0))
            wide_ref[slot, q, :, SIDE : 2 * SIDE] = both.astype(jnp.bfloat16)
        for q in range(ZPER):
            got = jnp.dot(
                wide_ref[slot, q], wx_ref[...], preferred_element_type=jnp.float32
            ).astype(jnp.bfloat16)
            for w in range(VIEWS):
                ax_ref[w, z0 + q] = got[:, w * SIDE : (w + 1) * SIDE]


def filter_y(v, wy_ref, ax_ref, ay_ref):
    @pl.loop(0, CZ // 2, unroll=UY)
    def _(i):
        pair = jnp.concatenate([ax_ref[v, 2 * i], ax_ref[v, 2 * i + 1]], axis=1)
        got = jnp.dot(wy_ref[0], pair, preferred_element_type=jnp.float32)
        ay_ref[:, i] = interleave(got).astype(jnp.bfloat16)


def filter_z(i, wz_ref, ay_ref):
    one = ay_ref[2 * i].reshape(CZ * HALF_TILE, SIDE)
    two = ay_ref[2 * i + 1].reshape(CZ * HALF_TILE, SIDE)
    return jnp.dot(
        wz_ref[0], jnp.concatenate([one, two], axis=1), preferred_element_type=jnp.float32
    )


def compare(i, blur, seen, count_ref, bz_ref, rz_ref):
    rows = pl.ds(pl.multiple_of(i * RIM, RIM), RIM)
    seen = side_by_side(seen.astype(jnp.float32))
    times = jnp.concatenate([count_ref[0], count_ref[0]], axis=1)
    ratio = ((seen + DAMPING) / (times * blur + DAMPING)).astype(jnp.bfloat16)
    back = jnp.dot(bz_ref[0], ratio, preferred_element_type=jnp.float32)
    rz_ref[:, rows, :] = interleave(back).astype(jnp.bfloat16)


def spread_y(v, by_ref, rz_ref, ry_ref):
    at = pl.ds(pl.multiple_of(v * SIDE, SIDE), SIDE)

    @pl.loop(0, CZ // 2, unroll=UB)
    def _(i):
        pair = jnp.concatenate([rz_ref[2 * i], rz_ref[2 * i + 1]], axis=1)
        got = jnp.dot(by_ref[0], pair, preferred_element_type=jnp.float32).astype(jnp.bfloat16)
        ry_ref[2 * i, :, at] = got[:, :SIDE]
        ry_ref[2 * i + 1, :, at] = got[:, SIDE:]


def spread_x(bx_ref, ry_ref, mid_ref, up_ref, down_ref, goleft_ref, goright_ref):
    @pl.loop(0, ZPER, unroll=UE)
    def _(q):
        goleft = jnp.zeros((EXT, SIDE), jnp.float32)
        goright = jnp.zeros((EXT, SIDE), jnp.float32)
        for g in range(GROUPS):
            z = g * ZPER + q
            got = jnp.dot(ry_ref[z], bx_ref[...], preferred_element_type=jnp.float32)
            up_ref[z] = got[:RIM, :SIDE]
            mid_ref[z] = got[RIM : RIM + SIDE, :SIDE]
            down_ref[z] = got[RIM + SIDE :, :SIDE]
            strip = got[:, SIDE:]
            mine = lanes((EXT, SIDE)) // RIM == g
            goleft = jnp.where(mine, pltpu.roll(strip, RIM * g, 1), goleft)
            goright = jnp.where(mine, pltpu.roll(strip, (SIDE + RIM * g - RIM) % SIDE, 1), goright)
        goleft_ref[q] = goleft
        goright_ref[q] = goright


def forward_body(
    est_ref, top_ref, bot_ref, left_ref, right_ref, wx_ref, wy_ref, wz_ref,
    blur_ref, wide_ref, ax_ref, ay_ref,
):
    v = pl.program_id(0)

    @pl.when(v == 0)
    def _():
        filter_x(est_ref, top_ref, bot_ref, left_ref, right_ref, wx_ref, wide_ref, ax_ref)

    filter_y(v, wy_ref, ax_ref, ay_ref)

    @pl.loop(0, SIDE // RIM, unroll=UZ)
    def _(i):
        blur_ref[0, i] = filter_z(i, wz_ref, ay_ref)


def backward_body(
    got_ref, blur_ref, bx_ref, by_ref, bz_ref,
    mid_ref, up_ref, down_ref, goleft_ref, goright_ref, obs_ref, count_ref,
    rz_ref, ry_ref, tiles_ref, names_ref, wide_ref, label_ref, head_ref, next_ref, times_ref,
    sems,
):
    v = pl.program_id(0)
    sources = got_ref.shape[0]

    @pl.when(v == 0)
    def _():
        names = pltpu.make_async_copy(
            got_ref.at[:, pl.ds(SLOTS * SIDE, HALF_TILE)], names_ref, sems.at[0]
        )
        tiles = pltpu.make_async_copy(
            got_ref.at[:, pl.ds(0, SLOTS * SIDE)], tiles_ref, sems.at[1]
        )
        names.start()
        tiles.start()

        @pl.loop(0, VIEWS * CZ, unroll=8)
        def _(i):
            head_ref[i] = 0
            times_ref[i] = 0

        names.wait()
        wide_ref[...] = names_ref[...].astype(jnp.float32)[:, 0, :].astype(jnp.int32)
        labels = pltpu.make_async_copy(wide_ref, label_ref, sems.at[2])
        labels.start()
        labels.wait()

        @pl.loop(0, sources)
        def _(i):
            for r in range(SLOTS):
                label = label_ref[i, r]

                @pl.when(label >= 0)
                def _():
                    next_ref[i * SLOTS + r] = head_ref[label]
                    head_ref[label] = i * SLOTS + r
                    times_ref[label] = times_ref[label] + 1

        tiles.wait()

    def tile(i):
        return tiles_ref[i // SLOTS, pl.ds(pl.multiple_of(i % SLOTS * SIDE, SIDE), SIDE)]

    @pl.loop(0, CZ, unroll=4)
    def _(z):
        first = head_ref[v * CZ + z]
        times = times_ref[v * CZ + z]
        count_ref[0, pl.ds(pl.multiple_of(z * HALF_TILE, HALF_TILE), HALF_TILE)] = jnp.full(
            (HALF_TILE, SIDE), times.astype(jnp.float32)
        )
        obs_ref[0, z] = jnp.where(times > 0, tile(first), jnp.zeros((), jnp.bfloat16))

    @pl.loop(0, CZ)
    def _(z):
        times = times_ref[v * CZ + z]

        @pl.when(times > 1)
        def _():
            def add(_, carry):
                at, total = carry
                return next_ref[at], total + tile(at).astype(jnp.float32)

            first = head_ref[v * CZ + z]
            total = jnp.zeros((SIDE, SIDE), jnp.float32)
            obs_ref[0, z] = lax.fori_loop(0, times, add, (first, total))[1].astype(jnp.bfloat16)

    @pl.loop(0, SIDE // RIM, unroll=UZ)
    def _(i):
        rows = pl.ds(pl.multiple_of(i * RIM, RIM), RIM)
        compare(i, blur_ref[0, i], obs_ref[0, :, rows, :], count_ref, bz_ref, rz_ref)

    spread_y(v, by_ref, rz_ref, ry_ref)

    @pl.when(v == VIEWS - 1)
    def _():
        spread_x(bx_ref, ry_ref, mid_ref, up_ref, down_ref, goleft_ref, goright_ref)


def step_body(
    est_ref, top_ref, bot_ref, left_ref, right_ref, obs_ref, count_ref,
    wx_ref, wy_ref, wz_ref, bx_ref, by_ref, bz_ref,
    mid_ref, up_ref, down_ref, goleft_ref, goright_ref,
    wide_ref, ax_ref, ay_ref, rz_ref, ry_ref,
):
    v = pl.program_id(0)

    @pl.when(v == 0)
    def _():
        filter_x(est_ref, top_ref, bot_ref, left_ref, right_ref, wx_ref, wide_ref, ax_ref)

    filter_y(v, wy_ref, ax_ref, ay_ref)

    @pl.loop(0, SIDE // RIM, unroll=UZ)
    def _(i):
        rows = pl.ds(pl.multiple_of(i * RIM, RIM), RIM)
        blur = filter_z(i, wz_ref, ay_ref)
        compare(i, blur, obs_ref[0, :, rows, :], count_ref, bz_ref, rz_ref)

    spread_y(v, by_ref, rz_ref, ry_ref)

    @pl.when(v == VIEWS - 1)
    def _():
        spread_x(bx_ref, ry_ref, mid_ref, up_ref, down_ref, goleft_ref, goright_ref)


def whole(*shape):
    return pl.BlockSpec(shape, lambda v, *_: (0,) * len(shape))


def once(*shape):
    return pl.BlockSpec(
        shape, lambda v, *_: (0,) * len(shape), pipeline_mode=pl.Buffered(1)
    )


def per_view(*shape):
    return pl.BlockSpec((1,) + shape, lambda v, *_: (v,) + (0,) * len(shape))


ROWS = (CZ, RIM, SIDE)
CORE = (CZ, SIDE, SIDE)
STRIP = (ZPER, EXT, SIDE)
Z_BAND = (CZ * HALF_TILE, CZ * HALF_TILE)
TIMES = (CZ * HALF_TILE, SIDE)
BLUR = (SIDE // RIM, CZ * HALF_TILE, 2 * SIDE)
HALO_SPECS = [once(*ROWS), once(*ROWS), once(*STRIP), once(*STRIP)]
FRONT_SPECS = [once(2 * SIDE, VIEWS * SIDE), per_view(SIDE, EXT), per_view(*Z_BAND)]
BACK_SPECS = [once(VIEWS * SIDE, 2 * SIDE), per_view(EXT, SIDE), per_view(*Z_BAND)]
PART_SPECS = [whole(*CORE), whole(*ROWS), whole(*ROWS), whole(*STRIP), whole(*STRIP)]
PARTS = tuple(
    jax.ShapeDtypeStruct(shape, jnp.float32) for shape in (CORE, ROWS, ROWS, STRIP, STRIP)
)
FRONT_SCRATCH = [
    pltpu.VMEM((UX, ZPER, EXT, 2 * SIDE), jnp.bfloat16),
    pltpu.VMEM((VIEWS, CZ, EXT, SIDE), jnp.bfloat16),
    pltpu.VMEM((SIDE // HALF_TILE, CZ // 2, RIM, SIDE), jnp.bfloat16),
]
BACK_SCRATCH = [
    pltpu.VMEM(CORE, jnp.bfloat16),
    pltpu.VMEM((CZ, EXT, VIEWS * SIDE), jnp.bfloat16),
]


def forward(est, halo, weights):
    return pl.pallas_call(
        forward_body,
        out_shape=jax.ShapeDtypeStruct((VIEWS,) + BLUR, jnp.float32),
        grid=(VIEWS,),
        in_specs=[once(*CORE)] + HALO_SPECS + FRONT_SPECS,
        out_specs=per_view(*BLUR),
        scratch_shapes=FRONT_SCRATCH,
        compiler_params=room(30),
        name="forward",
    )(est, *halo, *weights[:3])


def backward(got, blur, weights):
    sources = got.shape[0]
    return pl.pallas_call(
        backward_body,
        out_shape=PARTS
        + (
            jax.ShapeDtypeStruct((VIEWS,) + CORE, jnp.bfloat16),
            jax.ShapeDtypeStruct((VIEWS,) + TIMES, jnp.float32),
        ),
        grid=(VIEWS,),
        in_specs=[pl.BlockSpec(memory_space=pl.ANY), per_view(*BLUR)] + BACK_SPECS,
        out_specs=PART_SPECS + [per_view(*CORE), per_view(*TIMES)],
        scratch_shapes=BACK_SCRATCH
        + [
            pltpu.VMEM((sources, SLOTS * SIDE, SIDE), jnp.bfloat16),
            pltpu.VMEM((sources, HALF_TILE, SIDE), jnp.bfloat16),
            pltpu.VMEM((sources, SIDE), jnp.int32),
            pltpu.SMEM((sources, SIDE), jnp.int32),
            pltpu.SMEM((VIEWS * CZ,), jnp.int32),
            pltpu.SMEM((sources * SLOTS,), jnp.int32),
            pltpu.SMEM((VIEWS * CZ,), jnp.int32),
            pltpu.SemaphoreType.DMA((3,)),
        ],
        compiler_params=room(38),
        name="backward",
    )(got, blur, *weights[3:])


def iterate(counted, est, halo, observed, weights):
    return pl.pallas_call(
        step_body,
        out_shape=PARTS,
        grid=(VIEWS,),
        in_specs=[once(*CORE)]
        + HALO_SPECS
        + [per_view(*CORE), per_view(*TIMES)]
        + FRONT_SPECS
        + BACK_SPECS,
        out_specs=PART_SPECS,
        scratch_shapes=FRONT_SCRATCH + BACK_SCRATCH,
        compiler_params=room(38),
        name="iterate",
    )(est, *halo, observed, counted, *weights)


def beside(q, g, rows, left_ref, right_ref):
    low = pltpu.roll(left_ref[q, rows], (SIDE - RIM * g) % SIDE, 1)
    high = pltpu.roll(right_ref[q, rows], (2 * SIDE - RIM - RIM * g) % SIDE, 1)
    lane = lanes(low.shape)
    return jnp.where(lane < RIM, low, jnp.where(lane >= SIDE - RIM, high, 0.0))


def in_two(values):
    high = values.astype(jnp.bfloat16)
    return high, (values - high.astype(jnp.float32)).astype(jnp.bfloat16)


def join_x_body(first_ref, last_ref, up_ref, down_ref, left_ref, right_ref, *outs):
    @pl.loop(0, ZPER, unroll=True)
    def _(q):
        for g in range(GROUPS):
            z = g * ZPER + q
            head = up_ref[z] + beside(q, g, slice(0, RIM), left_ref, right_ref)
            tail = down_ref[z] + beside(q, g, slice(SIDE + RIM, EXT), left_ref, right_ref)
            outs[0][z], outs[1][z] = head, tail
            if len(outs) > 2:
                own = first_ref[z] + beside(q, g, slice(RIM, 2 * RIM), left_ref, right_ref)
                outs[2][z], outs[2][CZ + z] = in_two(head)
                outs[2][2 * CZ + z] = own.astype(jnp.bfloat16)
                own = last_ref[z] + beside(q, g, slice(SIDE, SIDE + RIM), left_ref, right_ref)
                outs[3][z], outs[3][CZ + z] = in_two(tail)
                outs[3][2 * CZ + z] = own.astype(jnp.bfloat16)


def join_x(mid, up, down, from_left, from_right, more):
    rows = jax.ShapeDtypeStruct(ROWS, jnp.float32)
    message = jax.ShapeDtypeStruct((3 * CZ, RIM, SIDE), jnp.bfloat16)
    out_shape = (rows, rows) + ((message, message) if more else ())
    return pl.pallas_call(
        join_x_body,
        out_shape=out_shape,
        grid=(1,),
        in_specs=[
            pl.BlockSpec(ROWS, lambda i: (0, 0, 0)),
            pl.BlockSpec(ROWS, lambda i: (0, SIDE // RIM - 1, 0)),
            whole(*ROWS),
            whole(*ROWS),
            whole(*STRIP),
            whole(*STRIP),
        ],
        out_specs=[whole(*shape.shape) for shape in out_shape],
        compiler_params=room(12),
        name="join_x",
    )(mid, mid, up, down, from_left, from_right)


def joined(est_ref, mid_ref, left_ref, right_ref, q, g, head, tail):
    z = g * ZPER + q
    total = mid_ref[z] + beside(q, g, slice(RIM, RIM + SIDE), left_ref, right_ref)
    total = jnp.concatenate(
        [total[:RIM] + head, total[RIM : SIDE - RIM], total[SIDE - RIM :] + tail], axis=0
    )
    return est_ref[z] * total / VIEWS


def last_join_body(est_ref, mid_ref, left_ref, right_ref, above_ref, below_ref, out_ref):
    @pl.loop(0, ZPER, unroll=2)
    def _(q):
        for g in range(GROUPS):
            z = g * ZPER + q
            out_ref[z] = joined(
                est_ref, mid_ref, left_ref, right_ref, q, g, above_ref[z], below_ref[z]
            )


def last_join(est, mid, from_left, from_right, above, below):
    return pl.pallas_call(
        last_join_body,
        out_shape=jax.ShapeDtypeStruct(CORE, jnp.float32),
        compiler_params=room(20),
        name="last_join",
    )(est, mid, from_left, from_right, above, below)


def cut(q, planes, left_ref, right_ref):
    low = jnp.zeros((EXT, SIDE), jnp.float32)
    high = jnp.zeros((EXT, SIDE), jnp.float32)
    for g, plane in enumerate(planes):
        mine = lanes((EXT, SIDE)) // RIM == g
        low = jnp.where(mine, pltpu.roll(plane, RIM * g, 1), low)
        high = jnp.where(mine, pltpu.roll(plane, (RIM * g + RIM) % SIDE, 1), high)
    left_ref[q] = low.astype(jnp.bfloat16)
    right_ref[q] = high.astype(jnp.bfloat16)


def next_join_body(
    est_ref, mid_ref, left_ref, right_ref, above_ref, below_ref,
    up_ref, down_ref, top_ref, bot_ref,
    out_ref, newtop_ref, newbot_ref, goleft_ref, goright_ref,
):
    def whole_of(ref, z):
        return ref[z].astype(jnp.float32) + ref[CZ + z].astype(jnp.float32)

    @pl.loop(0, ZPER, unroll=2)
    def _(q):
        planes = []
        for g in range(GROUPS):
            z = g * ZPER + q
            now = joined(
                est_ref, mid_ref, left_ref, right_ref, q, g,
                whole_of(above_ref, z), whole_of(below_ref, z),
            )
            out_ref[z] = now
            total = above_ref[2 * CZ + z].astype(jnp.float32) + up_ref[z]
            newtop = top_ref[z].astype(jnp.float32) * total / VIEWS
            newtop_ref[z] = newtop.astype(jnp.bfloat16)
            total = below_ref[2 * CZ + z].astype(jnp.float32) + down_ref[z]
            newbot = bot_ref[z].astype(jnp.float32) * total / VIEWS
            newbot_ref[z] = newbot.astype(jnp.bfloat16)
            planes.append(jnp.concatenate([newtop, now, newbot], axis=0))
        cut(q, planes, goleft_ref, goright_ref)


def next_join(est, mid, from_left, from_right, above, below, up, down, top, bot):
    rows = jax.ShapeDtypeStruct(ROWS, jnp.bfloat16)
    strip = jax.ShapeDtypeStruct(STRIP, jnp.bfloat16)
    return pl.pallas_call(
        next_join_body,
        out_shape=(jax.ShapeDtypeStruct(CORE, jnp.float32), rows, rows, strip, strip),
        compiler_params=room(24),
        name="next_join",
    )(est, mid, from_left, from_right, above, below, up, down, top, bot)


def rims_body(first_ref, last_ref, top_ref, bot_ref):
    top_ref[...] = first_ref[...].astype(jnp.bfloat16)
    bot_ref[...] = last_ref[...].astype(jnp.bfloat16)


def rims(est):
    rows = jax.ShapeDtypeStruct(ROWS, jnp.bfloat16)
    return pl.pallas_call(
        rims_body,
        out_shape=(rows, rows),
        grid=(1,),
        in_specs=[
            pl.BlockSpec(ROWS, lambda i: (0, 0, 0)),
            pl.BlockSpec(ROWS, lambda i: (0, SIDE // RIM - 1, 0)),
        ],
        out_specs=[whole(*ROWS), whole(*ROWS)],
        compiler_params=room(8),
        name="rims",
    )(est, est)


def edges_body(est_ref, top_ref, bot_ref, left_ref, right_ref):
    @pl.loop(0, ZPER, unroll=2)
    def _(q):
        planes = []
        for g in range(GROUPS):
            z = g * ZPER + q
            rim = (top_ref[z].astype(jnp.float32), bot_ref[z].astype(jnp.float32))
            planes.append(jnp.concatenate([rim[0], est_ref[z], rim[1]], axis=0))
        cut(q, planes, left_ref, right_ref)


def edges(est, top, bot):
    strip = jax.ShapeDtypeStruct(STRIP, jnp.bfloat16)
    return pl.pallas_call(
        edges_body,
        out_shape=(strip, strip),
        compiler_params=room(12),
        name="edges",
    )(est, top, bot)


def pick(taps, offset):
    hot = (offset[:, :, None] == jnp.arange(TAPS)[None, None, :]).astype(jnp.bfloat16)
    return jnp.einsum("rct,vt->vrc", hot, taps, preferred_element_type=jnp.float32).astype(
        jnp.bfloat16
    )


def weights_of(psf):
    kernel = (psf / jnp.sum(psf, axis=2, keepdims=True)).astype(jnp.bfloat16)
    core = jnp.arange(SIDE)
    rim = jnp.arange(RIM)
    far = jnp.full((SIDE - 2 * RIM,), 4 * SIDE)
    where_x = jnp.concatenate([core, rim - RIM, SIDE + rim, far])
    wx = pick(kernel[:, 2], where_x[:, None] - core[None, :] + REACH)
    wx = jnp.transpose(wx, (1, 0, 2)).reshape(2 * SIDE, VIEWS * SIDE)
    bx = pick(kernel[:, 2], where_x[None, :] - core[:, None] + REACH).reshape(
        VIEWS * SIDE, 2 * SIDE
    )
    where_y = jnp.arange(EXT) - RIM
    wy = pick(kernel[:, 1], where_y[None, :] - core[:, None] + REACH)
    by = pick(kernel[:, 1], where_y[:, None] - core[None, :] + REACH)
    row = jnp.arange(CZ * HALF_TILE)
    same = row[:, None] % HALF_TILE == row[None, :] % HALF_TILE
    gap = row[None, :] // HALF_TILE - row[:, None] // HALF_TILE
    wz = pick(kernel[:, 0], jnp.where(same, gap + REACH, -1))
    bz = pick(kernel[:, 0], jnp.where(same, REACH - gap, -1))
    return wx, wy, wz, bx, by, bz


def local(tiles, tile_dest, tile_slot, psf, estimate):
    axes = ("gy", "gx")
    devices = lax.axis_size("gy") * lax.axis_size("gx")
    first_rows, last_rows = rims(estimate)
    top, bot = shift(last_rows, "gy", 1), shift(first_rows, "gy", -1)
    dest = tile_dest[:, 0]
    count = dest.shape[0]
    order = (jnp.arange(count) * 256 + tile_slot)[None, :]
    hit = dest[None, :] == jnp.arange(devices)[:, None]
    first = jnp.min(jnp.where(hit, order, count * 256), axis=1)[:, None, None]
    last = jnp.max(jnp.where(hit, order, -1), axis=1)[:, None, None]
    one = jnp.where(first < count * 256, first % 256, -1)
    two = jnp.where(last > first, last % 256, -1)
    labels = jnp.where(lanes((devices, HALF_TILE, SIDE)) == 0, one, two).astype(jnp.bfloat16)
    low, high = edges(estimate, top, bot)
    left, right = shift(high, "gx", 1), shift(low, "gx", -1)
    packed = pack(dest, tiles, labels)
    packed, left, right = lax.optimization_barrier((packed, left, right))
    got = lax.all_to_all(packed, axes, split_axis=0, concat_axis=0, tiled=True)
    weights = weights_of(psf)
    blur = forward(estimate, (top, bot, left, right), weights)
    *parts, observed, counted = backward(got, blur, weights)
    for repeat_index in range(ITERS):
        more = repeat_index + 1 < ITERS
        mid, up, down, goleft, goright = parts
        sides = shift(goright, "gx", 1), shift(goleft, "gx", -1)
        sent = join_x(mid, up, down, *sides, more)
        if not more:
            up, down = sent
            return last_join(
                estimate, mid, *sides, shift(down, "gy", 1), shift(up, "gy", -1)
            )
        up, down, goup, godown = sent
        estimate, top, bot, low, high = next_join(
            estimate, mid, *sides, shift(godown, "gy", 1), shift(goup, "gy", -1), up, down, top, bot
        )
        halo = top, bot, shift(high, "gx", 1), shift(low, "gx", -1)
        parts = iterate(counted, estimate, halo, observed, weights)


def solution(mesh):
    placed = (
        P(("gy", "gx"), None, None),
        P(("gy", "gx"), None),
        P(("gy", "gx")),
        P(),
        P(None, "gy", "gx"),
    )
    return jax.shard_map(
        local, mesh=mesh, in_specs=placed, out_specs=P(None, "gy", "gx"), check_vma=False
    )
```

```python
import jax
import jax.numpy as jnp
from jax import lax
from jax.experimental import pallas as pl
from jax.experimental.pallas import tpu as pltpu
from jax.sharding import PartitionSpec as P

ITERS = 2
DAMPING = 0.05
VIEWS = 6
TAPS = 31
REACH = 15
CZ = 32
SIDE = 128
RIM = 16
EXT = SIDE + 2 * RIM
GROUPS = SIDE // RIM
ZPER = CZ // GROUPS
SLOTS = 2
HALF_TILE = 8
UX, UY, UZ, UB, UE = 2, 16, 8, 16, 2
def room(mebibytes):
    return pltpu.CompilerParams(vmem_limit_bytes=mebibytes << 20)


def shift(values, axis, step):
    count = lax.axis_size(axis)
    pairs = [(i, i + step) for i in range(count) if 0 <= i + step < count]
    return lax.ppermute(values, axis, pairs)


def lanes(shape):
    return lax.broadcasted_iota(jnp.int32, shape, len(shape) - 1)


def pack_body(dest_ref, tiles_ref, labels_ref, out_ref, seen_ref, tile_sem, label_sem):
    count = tiles_ref.shape[0]
    devices = out_ref.shape[0]
    named = pltpu.make_async_copy(
        labels_ref, out_ref.at[:, pl.ds(SLOTS * SIDE, HALF_TILE)], label_sem
    )
    named.start()

    @pl.loop(0, devices)
    def _(i):
        seen_ref[i] = 0

    @pl.loop(0, count)
    def _(i):
        target = dest_ref[i]
        rank = seen_ref[target]
        seen_ref[target] = rank + 1
        pltpu.make_async_copy(
            tiles_ref.at[i], out_ref.at[target, pl.ds(rank * SIDE, SIDE)], tile_sem
        ).start()

    every = out_ref.at[pl.ds(0, count // SLOTS), pl.ds(0, SLOTS * SIDE)]
    pltpu.make_async_copy(every, every, tile_sem).wait()
    named.wait()


def pack(tile_dest, tiles, labels):
    devices = labels.shape[0]
    return pl.pallas_call(
        pack_body,
        out_shape=jax.ShapeDtypeStruct((devices, SLOTS * SIDE + HALF_TILE, SIDE), tiles.dtype),
        in_specs=[
            pl.BlockSpec(memory_space=pltpu.SMEM),
            pl.BlockSpec(memory_space=pltpu.VMEM),
            pl.BlockSpec(memory_space=pltpu.VMEM),
        ],
        out_specs=pl.BlockSpec(memory_space=pltpu.HBM),
        scratch_shapes=[
            pltpu.SMEM((devices,), jnp.int32),
            pltpu.SemaphoreType.DMA(()),
            pltpu.SemaphoreType.DMA(()),
        ],
        compiler_params=room(56),
        name="pack",
    )(tile_dest, tiles, labels)


TOP_CODE = 32767
KNEE = 8.0


def encode(sums):
    code = (sums / (sums + KNEE) * TOP_CODE + 0.5).astype(jnp.int32)
    return jnp.minimum(code, TOP_CODE - 1).astype(jnp.int16)


def decode(codes):
    codes = codes.astype(jnp.int32).astype(jnp.float32)
    return KNEE * codes / (TOP_CODE - codes)


def side_by_side(pair):
    return jnp.concatenate([pair[:, :HALF_TILE], pair[:, HALF_TILE:]], axis=2).reshape(
        -1, 2 * SIDE
    )


def interleave(wide):
    wide = wide.reshape(-1, HALF_TILE, 2 * SIDE)
    return jnp.concatenate([wide[:, :, :SIDE], wide[:, :, SIDE:]], axis=1)


def filter_x(est_ref, top_ref, bot_ref, left_ref, right_ref, wx_ref, wide_ref, ax_ref):
    @pl.loop(0, GROUPS, unroll=UX)
    def _(g):
        z0 = g * ZPER
        slot = g % UX
        wide_ref[slot, :, RIM : RIM + SIDE, 0:SIDE] = est_ref[pl.ds(z0, ZPER)].astype(
            jnp.bfloat16
        )
        wide_ref[slot, :, 0:RIM, 0:SIDE] = top_ref[pl.ds(z0, ZPER)]
        wide_ref[slot, :, RIM + SIDE : EXT, 0:SIDE] = bot_ref[pl.ds(z0, ZPER)]
        for q in range(ZPER):
            lane = lanes((EXT, SIDE))
            lo = pltpu.roll(left_ref[q].astype(jnp.float32), (SIDE - RIM * g) % SIDE, 1)
            hi = pltpu.roll(right_ref[q].astype(jnp.float32), (SIDE + RIM - RIM * g) % SIDE, 1)
            both = jnp.where(lane < RIM, lo, jnp.where(lane < 2 * RIM, hi, 0.0))
            wide_ref[slot, q, :, SIDE : 2 * SIDE] = both.astype(jnp.bfloat16)
        for q in range(ZPER):
            got = jnp.dot(
                wide_ref[slot, q], wx_ref[...], preferred_element_type=jnp.float32
            ).astype(jnp.bfloat16)
            for w in range(VIEWS):
                ax_ref[w, z0 + q] = got[:, w * SIDE : (w + 1) * SIDE]


def filter_y(v, wy_ref, ax_ref, ay_ref):
    @pl.loop(0, CZ // 2, unroll=UY)
    def _(i):
        pair = jnp.concatenate([ax_ref[v, 2 * i], ax_ref[v, 2 * i + 1]], axis=1)
        got = jnp.dot(wy_ref[0], pair, preferred_element_type=jnp.float32)
        ay_ref[:, i] = interleave(got).astype(jnp.bfloat16)


def filter_z(i, wz_ref, ay_ref):
    one = ay_ref[2 * i].reshape(CZ * HALF_TILE, SIDE)
    two = ay_ref[2 * i + 1].reshape(CZ * HALF_TILE, SIDE)
    return jnp.dot(
        wz_ref[0], jnp.concatenate([one, two], axis=1), preferred_element_type=jnp.float32
    )


def compare(i, blur, seen, count_ref, bz_ref, rz_ref):
    rows = pl.ds(pl.multiple_of(i * RIM, RIM), RIM)
    seen = side_by_side(seen.astype(jnp.float32))
    times = jnp.concatenate([count_ref[0], count_ref[0]], axis=1)
    ratio = ((seen + DAMPING) / (times * blur + DAMPING)).astype(jnp.bfloat16)
    back = jnp.dot(bz_ref[0], ratio, preferred_element_type=jnp.float32)
    rz_ref[:, rows, :] = interleave(back).astype(jnp.bfloat16)


def spread_y(v, by_ref, rz_ref, ry_ref):
    at = pl.ds(pl.multiple_of(v * SIDE, SIDE), SIDE)

    @pl.loop(0, CZ // 2, unroll=UB)
    def _(i):
        pair = jnp.concatenate([rz_ref[2 * i], rz_ref[2 * i + 1]], axis=1)
        got = jnp.dot(by_ref[0], pair, preferred_element_type=jnp.float32).astype(jnp.bfloat16)
        ry_ref[2 * i, :, at] = got[:, :SIDE]
        ry_ref[2 * i + 1, :, at] = got[:, SIDE:]


def spread_x(bx_ref, ry_ref, mid_ref, up_ref, down_ref, goleft_ref, goright_ref):
    @pl.loop(0, ZPER, unroll=UE)
    def _(q):
        goleft = jnp.zeros((EXT, SIDE), jnp.float32)
        goright = jnp.zeros((EXT, SIDE), jnp.float32)
        for g in range(GROUPS):
            z = g * ZPER + q
            got = jnp.dot(ry_ref[z], bx_ref[...], preferred_element_type=jnp.float32)
            up_ref[z] = got[:RIM, :SIDE]
            mid_ref[z] = got[RIM : RIM + SIDE, :SIDE]
            down_ref[z] = got[RIM + SIDE :, :SIDE]
            strip = got[:, SIDE:]
            mine = lanes((EXT, SIDE)) // RIM == g
            goleft = jnp.where(mine, pltpu.roll(strip, RIM * g, 1), goleft)
            goright = jnp.where(mine, pltpu.roll(strip, (SIDE + RIM * g - RIM) % SIDE, 1), goright)
        goleft_ref[q] = encode(goleft)
        goright_ref[q] = encode(goright)


def forward_body(
    est_ref, top_ref, bot_ref, left_ref, right_ref, wx_ref, wy_ref, wz_ref,
    blur_ref, wide_ref, ax_ref, ay_ref,
):
    v = pl.program_id(0)

    @pl.when(v == 0)
    def _():
        filter_x(est_ref, top_ref, bot_ref, left_ref, right_ref, wx_ref, wide_ref, ax_ref)

    filter_y(v, wy_ref, ax_ref, ay_ref)

    @pl.loop(0, SIDE // RIM, unroll=UZ)
    def _(i):
        blur_ref[0, i] = filter_z(i, wz_ref, ay_ref)


def backward_body(
    got_ref, blur_ref, bx_ref, by_ref, bz_ref,
    mid_ref, up_ref, down_ref, goleft_ref, goright_ref, obs_ref, count_ref,
    rz_ref, ry_ref, tiles_ref, names_ref, wide_ref, label_ref, head_ref, next_ref, times_ref,
    many_ref, plane_ref, sems,
):
    v = pl.program_id(0)
    sources = got_ref.shape[0]

    @pl.when(v == 0)
    def _():
        names = pltpu.make_async_copy(
            got_ref.at[:, pl.ds(SLOTS * SIDE, HALF_TILE)], names_ref, sems.at[0]
        )
        tiles = pltpu.make_async_copy(
            got_ref.at[:, pl.ds(0, SLOTS * SIDE)], tiles_ref, sems.at[1]
        )
        names.start()
        tiles.start()

        @pl.loop(0, VIEWS * CZ, unroll=8)
        def _(i):
            head_ref[i] = 0
            times_ref[i] = 0

        head_ref[VIEWS * CZ] = 0
        times_ref[VIEWS * CZ] = 0
        for w in range(VIEWS):
            many_ref[w] = 0

        names.wait()
        wide_ref[...] = names_ref[...].astype(jnp.float32)[:, 0, :].astype(jnp.int32)
        labels = pltpu.make_async_copy(wide_ref, label_ref, sems.at[2])
        labels.start()
        labels.wait()

        @pl.loop(0, sources, unroll=2)
        def _(i):
            for r in range(SLOTS):
                name = label_ref[i, r]
                label = jnp.where(name < 0, VIEWS * CZ, name)
                times = times_ref[label]
                next_ref[i * SLOTS + r] = head_ref[label]
                head_ref[label] = i * SLOTS + r
                times_ref[label] = times + 1

                @pl.when((times == 1) & (name >= 0))
                def _():
                    view = label // CZ
                    many = many_ref[view]
                    plane_ref[view * CZ + many] = label
                    many_ref[view] = many + 1

        tiles.wait()

    def tile(i):
        return tiles_ref[i // SLOTS, pl.ds(pl.multiple_of(i % SLOTS * SIDE, SIDE), SIDE)]

    @pl.loop(0, CZ, unroll=4)
    def _(z):
        first = head_ref[v * CZ + z]
        times = times_ref[v * CZ + z]
        count_ref[0, pl.ds(pl.multiple_of(z * HALF_TILE, HALF_TILE), HALF_TILE)] = jnp.full(
            (HALF_TILE, SIDE), times.astype(jnp.float32)
        )
        obs_ref[0, z] = jnp.where(times > 0, tile(first), jnp.zeros((), jnp.bfloat16))

    @pl.loop(0, many_ref[v])
    def _(i):
        plane = plane_ref[v * CZ + i]

        def add(_, carry):
            at, total = carry
            return next_ref[at], total + tile(at).astype(jnp.float32)

        total = jnp.zeros((SIDE, SIDE), jnp.float32)
        total = lax.fori_loop(0, times_ref[plane], add, (head_ref[plane], total))[1]
        obs_ref[0, plane - v * CZ] = total.astype(jnp.bfloat16)

    @pl.loop(0, SIDE // RIM, unroll=UZ)
    def _(i):
        rows = pl.ds(pl.multiple_of(i * RIM, RIM), RIM)
        compare(i, blur_ref[0, i], obs_ref[0, :, rows, :], count_ref, bz_ref, rz_ref)

    spread_y(v, by_ref, rz_ref, ry_ref)

    @pl.when(v == VIEWS - 1)
    def _():
        spread_x(bx_ref, ry_ref, mid_ref, up_ref, down_ref, goleft_ref, goright_ref)


def step_body(
    est_ref, top_ref, bot_ref, left_ref, right_ref, obs_ref, count_ref,
    wx_ref, wy_ref, wz_ref, bx_ref, by_ref, bz_ref,
    mid_ref, up_ref, down_ref, goleft_ref, goright_ref,
    wide_ref, ax_ref, ay_ref, rz_ref, ry_ref,
):
    v = pl.program_id(0)

    @pl.when(v == 0)
    def _():
        filter_x(est_ref, top_ref, bot_ref, left_ref, right_ref, wx_ref, wide_ref, ax_ref)

    filter_y(v, wy_ref, ax_ref, ay_ref)

    @pl.loop(0, SIDE // RIM, unroll=UZ)
    def _(i):
        rows = pl.ds(pl.multiple_of(i * RIM, RIM), RIM)
        blur = filter_z(i, wz_ref, ay_ref)
        compare(i, blur, obs_ref[0, :, rows, :], count_ref, bz_ref, rz_ref)

    spread_y(v, by_ref, rz_ref, ry_ref)

    @pl.when(v == VIEWS - 1)
    def _():
        spread_x(bx_ref, ry_ref, mid_ref, up_ref, down_ref, goleft_ref, goright_ref)


def whole(*shape):
    return pl.BlockSpec(shape, lambda v, *_: (0,) * len(shape))


def once(*shape):
    return pl.BlockSpec(
        shape, lambda v, *_: (0,) * len(shape), pipeline_mode=pl.Buffered(1)
    )


def per_view(*shape):
    return pl.BlockSpec((1,) + shape, lambda v, *_: (v,) + (0,) * len(shape))


ROWS = (CZ, RIM, SIDE)
CORE = (CZ, SIDE, SIDE)
STRIP = (ZPER, EXT, SIDE)
Z_BAND = (CZ * HALF_TILE, CZ * HALF_TILE)
TIMES = (CZ * HALF_TILE, SIDE)
BLUR = (SIDE // RIM, CZ * HALF_TILE, 2 * SIDE)
HALO_SPECS = [once(*ROWS), once(*ROWS), once(*STRIP), once(*STRIP)]
FRONT_SPECS = [once(2 * SIDE, VIEWS * SIDE), per_view(SIDE, EXT), per_view(*Z_BAND)]
BACK_SPECS = [once(VIEWS * SIDE, 2 * SIDE), per_view(EXT, SIDE), per_view(*Z_BAND)]
PART_SPECS = [whole(*CORE), whole(*ROWS), whole(*ROWS), whole(*STRIP), whole(*STRIP)]
PARTS = tuple(jax.ShapeDtypeStruct(shape, jnp.float32) for shape in (CORE, ROWS, ROWS)) + (
    jax.ShapeDtypeStruct(STRIP, jnp.int16),
    jax.ShapeDtypeStruct(STRIP, jnp.int16),
)
FRONT_SCRATCH = [
    pltpu.VMEM((UX, ZPER, EXT, 2 * SIDE), jnp.bfloat16),
    pltpu.VMEM((VIEWS, CZ, EXT, SIDE), jnp.bfloat16),
    pltpu.VMEM((SIDE // HALF_TILE, CZ // 2, RIM, SIDE), jnp.bfloat16),
]
BACK_SCRATCH = [
    pltpu.VMEM(CORE, jnp.bfloat16),
    pltpu.VMEM((CZ, EXT, VIEWS * SIDE), jnp.bfloat16),
]


def forward(est, halo, weights):
    return pl.pallas_call(
        forward_body,
        out_shape=jax.ShapeDtypeStruct((VIEWS,) + BLUR, jnp.float32),
        grid=(VIEWS,),
        in_specs=[once(*CORE)] + HALO_SPECS + FRONT_SPECS,
        out_specs=per_view(*BLUR),
        scratch_shapes=FRONT_SCRATCH,
        compiler_params=room(30),
        name="forward",
    )(est, *halo, *weights[:3])


def backward(got, blur, weights):
    sources = got.shape[0]
    return pl.pallas_call(
        backward_body,
        out_shape=PARTS
        + (
            jax.ShapeDtypeStruct((VIEWS,) + CORE, jnp.bfloat16),
            jax.ShapeDtypeStruct((VIEWS,) + TIMES, jnp.float32),
        ),
        grid=(VIEWS,),
        in_specs=[pl.BlockSpec(memory_space=pl.ANY), per_view(*BLUR)] + BACK_SPECS,
        out_specs=PART_SPECS + [per_view(*CORE), per_view(*TIMES)],
        scratch_shapes=BACK_SCRATCH
        + [
            pltpu.VMEM((sources, SLOTS * SIDE, SIDE), jnp.bfloat16),
            pltpu.VMEM((sources, HALF_TILE, SIDE), jnp.bfloat16),
            pltpu.VMEM((sources, SIDE), jnp.int32),
            pltpu.SMEM((sources, SIDE), jnp.int32),
            pltpu.SMEM((VIEWS * CZ + 1,), jnp.int32),
            pltpu.SMEM((sources * SLOTS,), jnp.int32),
            pltpu.SMEM((VIEWS * CZ + 1,), jnp.int32),
            pltpu.SMEM((VIEWS,), jnp.int32),
            pltpu.SMEM((VIEWS * CZ,), jnp.int32),
            pltpu.SemaphoreType.DMA((3,)),
        ],
        compiler_params=room(38),
        name="backward",
    )(got, blur, *weights[3:])


def iterate(counted, est, halo, observed, weights):
    return pl.pallas_call(
        step_body,
        out_shape=PARTS,
        grid=(VIEWS,),
        in_specs=[once(*CORE)]
        + HALO_SPECS
        + [per_view(*CORE), per_view(*TIMES)]
        + FRONT_SPECS
        + BACK_SPECS,
        out_specs=PART_SPECS,
        scratch_shapes=FRONT_SCRATCH + BACK_SCRATCH,
        compiler_params=room(38),
        name="iterate",
    )(est, *halo, observed, counted, *weights)


def beside(q, g, rows, left_ref, right_ref):
    low = pltpu.roll(decode(left_ref[q, rows]), (SIDE - RIM * g) % SIDE, 1)
    high = pltpu.roll(decode(right_ref[q, rows]), (2 * SIDE - RIM - RIM * g) % SIDE, 1)
    lane = lanes(low.shape)
    return jnp.where(lane < RIM, low, jnp.where(lane >= SIDE - RIM, high, 0.0))


def join_x_body(first_ref, last_ref, up_ref, down_ref, left_ref, right_ref, *outs):
    goup_ref, godown_ref = outs[:2]

    @pl.loop(0, ZPER, unroll=True)
    def _(q):
        for g in range(GROUPS):
            z = g * ZPER + q
            head = up_ref[z] + beside(q, g, slice(0, RIM), left_ref, right_ref)
            tail = down_ref[z] + beside(q, g, slice(SIDE + RIM, EXT), left_ref, right_ref)
            goup_ref[z], godown_ref[z] = encode(head), encode(tail)
            if len(outs) > 2:
                outs[2][z], outs[3][z] = head, tail
                own = first_ref[z] + beside(q, g, slice(RIM, 2 * RIM), left_ref, right_ref)
                goup_ref[CZ + z] = encode(own)
                own = last_ref[z] + beside(q, g, slice(SIDE, SIDE + RIM), left_ref, right_ref)
                godown_ref[CZ + z] = encode(own)


def join_x(mid, up, down, from_left, from_right, more):
    rows = jax.ShapeDtypeStruct(ROWS, jnp.float32)
    message = jax.ShapeDtypeStruct(((1 + more) * CZ, RIM, SIDE), jnp.int16)
    out_shape = (message, message) + ((rows, rows) if more else ())
    return pl.pallas_call(
        join_x_body,
        out_shape=out_shape,
        grid=(1,),
        in_specs=[
            pl.BlockSpec(ROWS, lambda i: (0, 0, 0)),
            pl.BlockSpec(ROWS, lambda i: (0, SIDE // RIM - 1, 0)),
            whole(*ROWS),
            whole(*ROWS),
            whole(*STRIP),
            whole(*STRIP),
        ],
        out_specs=[whole(*shape.shape) for shape in out_shape],
        compiler_params=room(12),
        name="join_x",
    )(mid, mid, up, down, from_left, from_right)


def joined(est_ref, mid_ref, left_ref, right_ref, q, g, head, tail):
    z = g * ZPER + q
    total = mid_ref[z] + beside(q, g, slice(RIM, RIM + SIDE), left_ref, right_ref)
    total = jnp.concatenate(
        [total[:RIM] + head, total[RIM : SIDE - RIM], total[SIDE - RIM :] + tail], axis=0
    )
    return est_ref[z] * total / VIEWS


def last_join_body(est_ref, mid_ref, left_ref, right_ref, above_ref, below_ref, out_ref):
    @pl.loop(0, ZPER, unroll=2)
    def _(q):
        for g in range(GROUPS):
            z = g * ZPER + q
            out_ref[z] = joined(
                est_ref, mid_ref, left_ref, right_ref, q, g,
                decode(above_ref[z]), decode(below_ref[z]),
            )


def last_join(est, mid, from_left, from_right, above, below):
    return pl.pallas_call(
        last_join_body,
        out_shape=jax.ShapeDtypeStruct(CORE, jnp.float32),
        compiler_params=room(20),
        name="last_join",
    )(est, mid, from_left, from_right, above, below)


def cut(q, planes, left_ref, right_ref):
    low = jnp.zeros((EXT, SIDE), jnp.float32)
    high = jnp.zeros((EXT, SIDE), jnp.float32)
    for g, plane in enumerate(planes):
        mine = lanes((EXT, SIDE)) // RIM == g
        low = jnp.where(mine, pltpu.roll(plane, RIM * g, 1), low)
        high = jnp.where(mine, pltpu.roll(plane, (RIM * g + RIM) % SIDE, 1), high)
    left_ref[q] = low.astype(jnp.bfloat16)
    right_ref[q] = high.astype(jnp.bfloat16)


def next_join_body(
    est_ref, mid_ref, left_ref, right_ref, above_ref, below_ref,
    up_ref, down_ref, top_ref, bot_ref,
    out_ref, newtop_ref, newbot_ref, goleft_ref, goright_ref,
):
    @pl.loop(0, ZPER, unroll=2)
    def _(q):
        planes = []
        for g in range(GROUPS):
            z = g * ZPER + q
            now = joined(
                est_ref, mid_ref, left_ref, right_ref, q, g,
                decode(above_ref[z]), decode(below_ref[z]),
            )
            out_ref[z] = now
            total = decode(above_ref[CZ + z]) + up_ref[z]
            newtop = top_ref[z].astype(jnp.float32) * total / VIEWS
            newtop_ref[z] = newtop.astype(jnp.bfloat16)
            total = decode(below_ref[CZ + z]) + down_ref[z]
            newbot = bot_ref[z].astype(jnp.float32) * total / VIEWS
            newbot_ref[z] = newbot.astype(jnp.bfloat16)
            planes.append(jnp.concatenate([newtop, now, newbot], axis=0))
        cut(q, planes, goleft_ref, goright_ref)


def next_join(est, mid, from_left, from_right, above, below, up, down, top, bot):
    rows = jax.ShapeDtypeStruct(ROWS, jnp.bfloat16)
    strip = jax.ShapeDtypeStruct(STRIP, jnp.bfloat16)
    return pl.pallas_call(
        next_join_body,
        out_shape=(jax.ShapeDtypeStruct(CORE, jnp.float32), rows, rows, strip, strip),
        compiler_params=room(24),
        name="next_join",
    )(est, mid, from_left, from_right, above, below, up, down, top, bot)


def rims_body(first_ref, last_ref, top_ref, bot_ref):
    top_ref[...] = first_ref[...].astype(jnp.bfloat16)
    bot_ref[...] = last_ref[...].astype(jnp.bfloat16)


def rims(est):
    rows = jax.ShapeDtypeStruct(ROWS, jnp.bfloat16)
    return pl.pallas_call(
        rims_body,
        out_shape=(rows, rows),
        grid=(1,),
        in_specs=[
            pl.BlockSpec(ROWS, lambda i: (0, 0, 0)),
            pl.BlockSpec(ROWS, lambda i: (0, SIDE // RIM - 1, 0)),
        ],
        out_specs=[whole(*ROWS), whole(*ROWS)],
        compiler_params=room(56),
        name="rims",
    )(est, est)


def edges_body(est_ref, top_ref, bot_ref, left_ref, right_ref):
    @pl.loop(0, ZPER, unroll=2)
    def _(q):
        planes = []
        for g in range(GROUPS):
            z = g * ZPER + q
            rim = (top_ref[z].astype(jnp.float32), bot_ref[z].astype(jnp.float32))
            planes.append(jnp.concatenate([rim[0], est_ref[z], rim[1]], axis=0))
        cut(q, planes, left_ref, right_ref)


def edges(est, top, bot):
    strip = jax.ShapeDtypeStruct(STRIP, jnp.bfloat16)
    return pl.pallas_call(
        edges_body,
        out_shape=(strip, strip),
        compiler_params=room(12),
        name="edges",
    )(est, top, bot)


def pick(taps, offset):
    hot = (offset[:, :, None] == jnp.arange(TAPS)[None, None, :]).astype(jnp.bfloat16)
    return jnp.einsum("rct,vt->vrc", hot, taps, preferred_element_type=jnp.float32).astype(
        jnp.bfloat16
    )


def weights_of(psf):
    kernel = (psf / jnp.sum(psf, axis=2, keepdims=True)).astype(jnp.bfloat16)
    core = jnp.arange(SIDE)
    rim = jnp.arange(RIM)
    far = jnp.full((SIDE - 2 * RIM,), 4 * SIDE)
    where_x = jnp.concatenate([core, rim - RIM, SIDE + rim, far])
    wx = pick(kernel[:, 2], where_x[:, None] - core[None, :] + REACH)
    wx = jnp.transpose(wx, (1, 0, 2)).reshape(2 * SIDE, VIEWS * SIDE)
    bx = pick(kernel[:, 2], where_x[None, :] - core[:, None] + REACH).reshape(
        VIEWS * SIDE, 2 * SIDE
    )
    where_y = jnp.arange(EXT) - RIM
    wy = pick(kernel[:, 1], where_y[None, :] - core[:, None] + REACH)
    by = pick(kernel[:, 1], where_y[:, None] - core[None, :] + REACH)
    row = jnp.arange(CZ * HALF_TILE)
    same = row[:, None] % HALF_TILE == row[None, :] % HALF_TILE
    gap = row[None, :] // HALF_TILE - row[:, None] // HALF_TILE
    wz = pick(kernel[:, 0], jnp.where(same, gap + REACH, -1))
    bz = pick(kernel[:, 0], jnp.where(same, REACH - gap, -1))
    return wx, wy, wz, bx, by, bz


def local(tiles, tile_dest, tile_slot, psf, estimate):
    axes = ("gy", "gx")
    devices = lax.axis_size("gy") * lax.axis_size("gx")
    first_rows, last_rows = rims(estimate)
    top, bot = shift(last_rows, "gy", 1), shift(first_rows, "gy", -1)
    dest = tile_dest[:, 0]
    count = dest.shape[0]
    order = (jnp.arange(count) * 256 + tile_slot)[None, :]
    hit = dest[None, :] == jnp.arange(devices)[:, None]
    first = jnp.min(jnp.where(hit, order, count * 256), axis=1)[:, None, None]
    last = jnp.max(jnp.where(hit, order, -1), axis=1)[:, None, None]
    one = jnp.where(first < count * 256, first % 256, -1)
    two = jnp.where(last > first, last % 256, -1)
    labels = jnp.where(lanes((devices, HALF_TILE, SIDE)) == 0, one, two).astype(jnp.bfloat16)
    labels, top, bot = lax.optimization_barrier((labels, top, bot))
    low, high = edges(estimate, top, bot)
    left, right = shift(high, "gx", 1), shift(low, "gx", -1)
    packed = pack(dest, tiles, labels)
    packed, left, right = lax.optimization_barrier((packed, left, right))
    got = lax.all_to_all(packed, axes, split_axis=0, concat_axis=0, tiled=True)
    weights = weights_of(psf)
    blur = forward(estimate, (top, bot, left, right), weights)
    *parts, observed, counted = backward(got, blur, weights)
    for repeat_index in range(ITERS):
        more = repeat_index + 1 < ITERS
        mid, up, down, goleft, goright = parts
        sides = shift(goright, "gx", 1), shift(goleft, "gx", -1)
        sent = join_x(mid, up, down, *sides, more)
        if not more:
            goup, godown = sent
            return last_join(
                estimate, mid, *sides, shift(godown, "gy", 1), shift(goup, "gy", -1)
            )
        goup, godown, up, down = sent
        estimate, top, bot, low, high = next_join(
            estimate, mid, *sides, shift(godown, "gy", 1), shift(goup, "gy", -1), up, down, top, bot
        )
        halo = top, bot, shift(high, "gx", 1), shift(low, "gx", -1)
        parts = iterate(counted, estimate, halo, observed, weights)


def solution(mesh):
    placed = (
        P(("gy", "gx"), None, None),
        P(("gy", "gx"), None),
        P(("gy", "gx")),
        P(),
        P(None, "gy", "gx"),
    )
    return jax.shard_map(
        local, mesh=mesh, in_specs=placed, out_specs=P(None, "gy", "gx"), check_vma=False
    )
```

```python
import jax
import jax.numpy as jnp
from jax import lax
from jax.experimental import pallas as pl
from jax.experimental.pallas import tpu as pltpu
from jax.sharding import PartitionSpec as P

ITERS = 2
DAMPING = 0.05
VIEWS = 6
TAPS = 31
REACH = 15
CZ = 32
SIDE = 128
RIM = 16
EXT = SIDE + 2 * RIM
GROUPS = SIDE // RIM
ZPER = CZ // GROUPS
SLOTS = 2
HALF_TILE = 8
UX, UY, UZ, UB, UE = 4, 16, 8, 16, 4
def room(mebibytes):
    return pltpu.CompilerParams(vmem_limit_bytes=mebibytes << 20)


def shift(values, axis, step):
    count = lax.axis_size(axis)
    pairs = [(i, i + step) for i in range(count) if 0 <= i + step < count]
    return lax.ppermute(values, axis, pairs)


def lanes(shape):
    return lax.broadcasted_iota(jnp.int32, shape, len(shape) - 1)


def pack_body(dest_ref, tiles_ref, labels_ref, out_ref, seen_ref, tile_sem, label_sem):
    count = tiles_ref.shape[0]
    devices = out_ref.shape[0]
    named = pltpu.make_async_copy(
        labels_ref, out_ref.at[:, pl.ds(SLOTS * SIDE, HALF_TILE)], label_sem
    )
    named.start()

    @pl.loop(0, devices)
    def _(i):
        seen_ref[i] = 0

    @pl.loop(0, count)
    def _(i):
        target = dest_ref[i]
        rank = seen_ref[target]
        seen_ref[target] = rank + 1
        pltpu.make_async_copy(
            tiles_ref.at[i], out_ref.at[target, pl.ds(rank * SIDE, SIDE)], tile_sem
        ).start()

    every = out_ref.at[pl.ds(0, count // SLOTS), pl.ds(0, SLOTS * SIDE)]
    pltpu.make_async_copy(every, every, tile_sem).wait()
    named.wait()


def pack(tile_dest, tiles, labels):
    devices = labels.shape[0]
    return pl.pallas_call(
        pack_body,
        out_shape=jax.ShapeDtypeStruct((devices, SLOTS * SIDE + HALF_TILE, SIDE), tiles.dtype),
        in_specs=[
            pl.BlockSpec(memory_space=pltpu.SMEM),
            pl.BlockSpec(memory_space=pltpu.VMEM),
            pl.BlockSpec(memory_space=pltpu.VMEM),
        ],
        out_specs=pl.BlockSpec(memory_space=pltpu.HBM),
        scratch_shapes=[
            pltpu.SMEM((devices,), jnp.int32),
            pltpu.SemaphoreType.DMA(()),
            pltpu.SemaphoreType.DMA(()),
        ],
        compiler_params=room(56),
        name="pack",
    )(tile_dest, tiles, labels)


TOP_CODE = 32767
KNEE = 8.0


def encode(sums):
    code = (sums / (sums + KNEE) * TOP_CODE + 0.5).astype(jnp.int32)
    return jnp.minimum(code, TOP_CODE - 1).astype(jnp.int16)


def decode(codes):
    codes = codes.astype(jnp.int32).astype(jnp.float32)
    return KNEE * codes / (TOP_CODE - codes)


def side_by_side(pair):
    return jnp.concatenate([pair[:, :HALF_TILE], pair[:, HALF_TILE:]], axis=2).reshape(
        -1, 2 * SIDE
    )


def interleave(wide):
    wide = wide.reshape(-1, HALF_TILE, 2 * SIDE)
    return jnp.concatenate([wide[:, :, :SIDE], wide[:, :, SIDE:]], axis=1)


def filter_x(est_ref, top_ref, bot_ref, left_ref, right_ref, wx_ref, wide_ref, ax_ref):
    @pl.loop(0, GROUPS, unroll=UX)
    def _(g):
        z0 = g * ZPER
        slot = g % UX
        wide_ref[slot, :, RIM : RIM + SIDE, 0:SIDE] = est_ref[pl.ds(z0, ZPER)].astype(
            jnp.bfloat16
        )
        wide_ref[slot, :, 0:RIM, 0:SIDE] = top_ref[pl.ds(z0, ZPER)]
        wide_ref[slot, :, RIM + SIDE : EXT, 0:SIDE] = bot_ref[pl.ds(z0, ZPER)]
        for q in range(ZPER):
            lane = lanes((EXT, SIDE))
            lo = pltpu.roll(left_ref[q].astype(jnp.float32), (SIDE - RIM * g) % SIDE, 1)
            hi = pltpu.roll(right_ref[q].astype(jnp.float32), (SIDE + RIM - RIM * g) % SIDE, 1)
            both = jnp.where(lane < RIM, lo, jnp.where(lane < 2 * RIM, hi, 0.0))
            wide_ref[slot, q, :, SIDE : 2 * SIDE] = both.astype(jnp.bfloat16)
        for q in range(ZPER):
            got = jnp.dot(
                wide_ref[slot, q], wx_ref[...], preferred_element_type=jnp.float32
            ).astype(jnp.bfloat16)
            for w in range(VIEWS):
                ax_ref[w, z0 + q] = got[:, w * SIDE : (w + 1) * SIDE]


def filter_y(v, wy_ref, ax_ref, ay_ref):
    @pl.loop(0, CZ // 2, unroll=UY)
    def _(i):
        pair = jnp.concatenate([ax_ref[v, 2 * i], ax_ref[v, 2 * i + 1]], axis=1)
        got = jnp.dot(wy_ref[0], pair, preferred_element_type=jnp.float32)
        ay_ref[:, i] = interleave(got).astype(jnp.bfloat16)


def filter_z(i, wz_ref, ay_ref):
    one = ay_ref[2 * i].reshape(CZ * HALF_TILE, SIDE)
    two = ay_ref[2 * i + 1].reshape(CZ * HALF_TILE, SIDE)
    return jnp.dot(
        wz_ref[0], jnp.concatenate([one, two], axis=1), preferred_element_type=jnp.float32
    )


def compare(i, blur, seen, count_ref, bz_ref, rz_ref):
    rows = pl.ds(pl.multiple_of(i * RIM, RIM), RIM)
    seen = side_by_side(seen.astype(jnp.float32))
    times = jnp.concatenate([count_ref[0], count_ref[0]], axis=1)
    ratio = ((seen + DAMPING) / (times * blur + DAMPING)).astype(jnp.bfloat16)
    back = jnp.dot(bz_ref[0], ratio, preferred_element_type=jnp.float32)
    rz_ref[:, rows, :] = interleave(back).astype(jnp.bfloat16)


def spread_y(v, by_ref, rz_ref, ry_ref):
    at = pl.ds(pl.multiple_of(v * SIDE, SIDE), SIDE)

    @pl.loop(0, CZ // 2, unroll=UB)
    def _(i):
        pair = jnp.concatenate([rz_ref[2 * i], rz_ref[2 * i + 1]], axis=1)
        got = jnp.dot(by_ref[0], pair, preferred_element_type=jnp.float32).astype(jnp.bfloat16)
        ry_ref[2 * i, :, at] = got[:, :SIDE]
        ry_ref[2 * i + 1, :, at] = got[:, SIDE:]


def spread_x(bx_ref, ry_ref, mid_ref, up_ref, down_ref, goleft_ref, goright_ref):
    @pl.loop(0, ZPER, unroll=UE)
    def _(q):
        goleft = jnp.zeros((EXT, SIDE), jnp.float32)
        goright = jnp.zeros((EXT, SIDE), jnp.float32)
        for g in range(GROUPS):
            z = g * ZPER + q
            got = jnp.dot(ry_ref[z], bx_ref[...], preferred_element_type=jnp.float32)
            up_ref[z] = got[:RIM, :SIDE]
            mid_ref[z] = got[RIM : RIM + SIDE, :SIDE]
            down_ref[z] = got[RIM + SIDE :, :SIDE]
            strip = got[:, SIDE:]
            mine = lanes((EXT, SIDE)) // RIM == g
            goleft = jnp.where(mine, pltpu.roll(strip, RIM * g, 1), goleft)
            goright = jnp.where(mine, pltpu.roll(strip, (SIDE + RIM * g - RIM) % SIDE, 1), goright)
        goleft_ref[q] = encode(goleft)
        goright_ref[q] = encode(goright)


def forward_body(
    est_ref, top_ref, bot_ref, left_ref, right_ref, wx_ref, wy_ref, wz_ref,
    blur_ref, wide_ref, ax_ref, ay_ref,
):
    v = pl.program_id(0)

    @pl.when(v == 0)
    def _():
        filter_x(est_ref, top_ref, bot_ref, left_ref, right_ref, wx_ref, wide_ref, ax_ref)

    filter_y(v, wy_ref, ax_ref, ay_ref)

    @pl.loop(0, SIDE // RIM, unroll=UZ)
    def _(i):
        blur_ref[0, i] = filter_z(i, wz_ref, ay_ref)


def backward_body(
    got_ref, blur_ref, bx_ref, by_ref, bz_ref,
    mid_ref, up_ref, down_ref, goleft_ref, goright_ref, obs_ref, count_ref,
    rz_ref, ry_ref, tiles_ref, names_ref, wide_ref, label_ref, head_ref, next_ref, times_ref,
    many_ref, plane_ref, sems,
):
    v = pl.program_id(0)
    sources = got_ref.shape[0]

    @pl.when(v == 0)
    def _():
        names = pltpu.make_async_copy(
            got_ref.at[:, pl.ds(SLOTS * SIDE, HALF_TILE)], names_ref, sems.at[0]
        )
        tiles = pltpu.make_async_copy(
            got_ref.at[:, pl.ds(0, SLOTS * SIDE)], tiles_ref, sems.at[1]
        )
        names.start()
        tiles.start()

        @pl.loop(0, VIEWS * CZ, unroll=8)
        def _(i):
            head_ref[i] = 0
            times_ref[i] = 0

        head_ref[VIEWS * CZ] = 0
        times_ref[VIEWS * CZ] = 0
        for w in range(VIEWS + 1):
            many_ref[w] = 0

        names.wait()
        wide_ref[...] = jnp.sum(names_ref[...].astype(jnp.float32), axis=0).astype(jnp.int32)
        labels = pltpu.make_async_copy(wide_ref, label_ref, sems.at[2])
        labels.start()
        labels.wait()

        @pl.loop(0, sources, unroll=8)
        def _(i):
            for r in range(SLOTS):
                name = label_ref[r, i] - 1
                label = jnp.where(name < 0, VIEWS * CZ, name)
                times = times_ref[label]
                next_ref[i * SLOTS + r] = head_ref[label]
                head_ref[label] = i * SLOTS + r
                times_ref[label] = times + 1
                view = label // CZ
                many = many_ref[view]
                plane_ref[view * (CZ + 1) + many] = label
                second = (times == 1) & (name >= 0)
                many_ref[view] = many + second.astype(jnp.int32)

        tiles.wait()

    def tile(i):
        return tiles_ref[i // SLOTS, pl.ds(pl.multiple_of(i % SLOTS * SIDE, SIDE), SIDE)]

    @pl.loop(0, CZ, unroll=16)
    def _(z):
        first = head_ref[v * CZ + z]
        times = times_ref[v * CZ + z]
        count_ref[0, pl.ds(pl.multiple_of(z * HALF_TILE, HALF_TILE), HALF_TILE)] = jnp.full(
            (HALF_TILE, SIDE), times.astype(jnp.float32)
        )
        obs_ref[0, z] = jnp.where(times > 0, tile(first), jnp.zeros((), jnp.bfloat16))

    @pl.loop(0, many_ref[v])
    def _(i):
        plane = plane_ref[v * (CZ + 1) + i]

        def add(_, carry):
            at, total = carry
            return next_ref[at], total + tile(at).astype(jnp.float32)

        total = jnp.zeros((SIDE, SIDE), jnp.float32)
        total = lax.fori_loop(0, times_ref[plane], add, (head_ref[plane], total))[1]
        obs_ref[0, plane - v * CZ] = total.astype(jnp.bfloat16)

    @pl.loop(0, SIDE // RIM, unroll=UZ)
    def _(i):
        rows = pl.ds(pl.multiple_of(i * RIM, RIM), RIM)
        compare(i, blur_ref[0, i], obs_ref[0, :, rows, :], count_ref, bz_ref, rz_ref)

    spread_y(v, by_ref, rz_ref, ry_ref)

    @pl.when(v == VIEWS - 1)
    def _():
        spread_x(bx_ref, ry_ref, mid_ref, up_ref, down_ref, goleft_ref, goright_ref)


def step_body(
    est_ref, top_ref, bot_ref, left_ref, right_ref, obs_ref, count_ref,
    wx_ref, wy_ref, wz_ref, bx_ref, by_ref, bz_ref,
    mid_ref, up_ref, down_ref, goleft_ref, goright_ref,
    wide_ref, ax_ref, ay_ref, rz_ref, ry_ref,
):
    v = pl.program_id(0)

    @pl.when(v == 0)
    def _():
        filter_x(est_ref, top_ref, bot_ref, left_ref, right_ref, wx_ref, wide_ref, ax_ref)

    filter_y(v, wy_ref, ax_ref, ay_ref)

    @pl.loop(0, SIDE // RIM, unroll=UZ)
    def _(i):
        rows = pl.ds(pl.multiple_of(i * RIM, RIM), RIM)
        blur = filter_z(i, wz_ref, ay_ref)
        compare(i, blur, obs_ref[0, :, rows, :], count_ref, bz_ref, rz_ref)

    spread_y(v, by_ref, rz_ref, ry_ref)

    @pl.when(v == VIEWS - 1)
    def _():
        spread_x(bx_ref, ry_ref, mid_ref, up_ref, down_ref, goleft_ref, goright_ref)


def whole(*shape):
    return pl.BlockSpec(shape, lambda v, *_: (0,) * len(shape))


def once(*shape):
    return pl.BlockSpec(
        shape, lambda v, *_: (0,) * len(shape), pipeline_mode=pl.Buffered(1)
    )


def per_view(*shape):
    return pl.BlockSpec((1,) + shape, lambda v, *_: (v,) + (0,) * len(shape))


ROWS = (CZ, RIM, SIDE)
CORE = (CZ, SIDE, SIDE)
STRIP = (ZPER, EXT, SIDE)
Z_BAND = (CZ * HALF_TILE, CZ * HALF_TILE)
TIMES = (CZ * HALF_TILE, SIDE)
BLUR = (SIDE // RIM, CZ * HALF_TILE, 2 * SIDE)
HALO_SPECS = [once(*ROWS), once(*ROWS), once(*STRIP), once(*STRIP)]
FRONT_SPECS = [once(2 * SIDE, VIEWS * SIDE), per_view(SIDE, EXT), per_view(*Z_BAND)]
BACK_SPECS = [once(VIEWS * SIDE, 2 * SIDE), per_view(EXT, SIDE), per_view(*Z_BAND)]
PART_SPECS = [whole(*CORE), whole(*ROWS), whole(*ROWS), whole(*STRIP), whole(*STRIP)]
PARTS = tuple(jax.ShapeDtypeStruct(shape, jnp.float32) for shape in (CORE, ROWS, ROWS)) + (
    jax.ShapeDtypeStruct(STRIP, jnp.int16),
    jax.ShapeDtypeStruct(STRIP, jnp.int16),
)
FRONT_SCRATCH = [
    pltpu.VMEM((UX, ZPER, EXT, 2 * SIDE), jnp.bfloat16),
    pltpu.VMEM((VIEWS, CZ, EXT, SIDE), jnp.bfloat16),
    pltpu.VMEM((SIDE // HALF_TILE, CZ // 2, RIM, SIDE), jnp.bfloat16),
]
BACK_SCRATCH = [
    pltpu.VMEM(CORE, jnp.bfloat16),
    pltpu.VMEM((CZ, EXT, VIEWS * SIDE), jnp.bfloat16),
]


def forward(est, halo, weights):
    return pl.pallas_call(
        forward_body,
        out_shape=jax.ShapeDtypeStruct((VIEWS,) + BLUR, jnp.float32),
        grid=(VIEWS,),
        in_specs=[once(*CORE)] + HALO_SPECS + FRONT_SPECS,
        out_specs=per_view(*BLUR),
        scratch_shapes=FRONT_SCRATCH,
        compiler_params=room(30),
        name="forward",
    )(est, *halo, *weights[:3])


def backward(got, blur, weights):
    sources = got.shape[0]
    return pl.pallas_call(
        backward_body,
        out_shape=PARTS
        + (
            jax.ShapeDtypeStruct((VIEWS,) + CORE, jnp.bfloat16),
            jax.ShapeDtypeStruct((VIEWS,) + TIMES, jnp.float32),
        ),
        grid=(VIEWS,),
        in_specs=[pl.BlockSpec(memory_space=pl.ANY), per_view(*BLUR)] + BACK_SPECS,
        out_specs=PART_SPECS + [per_view(*CORE), per_view(*TIMES)],
        scratch_shapes=BACK_SCRATCH
        + [
            pltpu.VMEM((sources, SLOTS * SIDE, SIDE), jnp.bfloat16),
            pltpu.VMEM((sources, HALF_TILE, SIDE), jnp.bfloat16),
            pltpu.VMEM((HALF_TILE, SIDE), jnp.int32),
            pltpu.SMEM((HALF_TILE, SIDE), jnp.int32),
            pltpu.SMEM((VIEWS * CZ + 1,), jnp.int32),
            pltpu.SMEM((sources * SLOTS,), jnp.int32),
            pltpu.SMEM((VIEWS * CZ + 1,), jnp.int32),
            pltpu.SMEM((VIEWS + 1,), jnp.int32),
            pltpu.SMEM(((VIEWS + 1) * (CZ + 1),), jnp.int32),
            pltpu.SemaphoreType.DMA((3,)),
        ],
        compiler_params=room(38),
        name="backward",
    )(got, blur, *weights[3:])


def iterate(counted, est, halo, observed, weights):
    return pl.pallas_call(
        step_body,
        out_shape=PARTS,
        grid=(VIEWS,),
        in_specs=[once(*CORE)]
        + HALO_SPECS
        + [per_view(*CORE), per_view(*TIMES)]
        + FRONT_SPECS
        + BACK_SPECS,
        out_specs=PART_SPECS,
        scratch_shapes=FRONT_SCRATCH + BACK_SCRATCH,
        compiler_params=room(38),
        name="iterate",
    )(est, *halo, observed, counted, *weights)


def beside(q, g, rows, left_ref, right_ref):
    low = pltpu.roll(decode(left_ref[q, rows]), (SIDE - RIM * g) % SIDE, 1)
    high = pltpu.roll(decode(right_ref[q, rows]), (2 * SIDE - RIM - RIM * g) % SIDE, 1)
    lane = lanes(low.shape)
    return jnp.where(lane < RIM, low, jnp.where(lane >= SIDE - RIM, high, 0.0))


def join_x_body(first_ref, last_ref, up_ref, down_ref, left_ref, right_ref, *outs):
    goup_ref, godown_ref = outs[:2]

    @pl.loop(0, ZPER, unroll=True)
    def _(q):
        for g in range(GROUPS):
            z = g * ZPER + q
            head = up_ref[z] + beside(q, g, slice(0, RIM), left_ref, right_ref)
            tail = down_ref[z] + beside(q, g, slice(SIDE + RIM, EXT), left_ref, right_ref)
            goup_ref[z], godown_ref[z] = encode(head), encode(tail)
            if len(outs) > 2:
                outs[2][z], outs[3][z] = head, tail
                own = first_ref[z] + beside(q, g, slice(RIM, 2 * RIM), left_ref, right_ref)
                goup_ref[CZ + z] = encode(own)
                own = last_ref[z] + beside(q, g, slice(SIDE, SIDE + RIM), left_ref, right_ref)
                godown_ref[CZ + z] = encode(own)


def join_x(mid, up, down, from_left, from_right, more):
    rows = jax.ShapeDtypeStruct(ROWS, jnp.float32)
    message = jax.ShapeDtypeStruct(((1 + more) * CZ, RIM, SIDE), jnp.int16)
    out_shape = (message, message) + ((rows, rows) if more else ())
    return pl.pallas_call(
        join_x_body,
        out_shape=out_shape,
        grid=(1,),
        in_specs=[
            pl.BlockSpec(ROWS, lambda i: (0, 0, 0)),
            pl.BlockSpec(ROWS, lambda i: (0, SIDE // RIM - 1, 0)),
            whole(*ROWS),
            whole(*ROWS),
            whole(*STRIP),
            whole(*STRIP),
        ],
        out_specs=[whole(*shape.shape) for shape in out_shape],
        compiler_params=room(12),
        name="join_x",
    )(mid, mid, up, down, from_left, from_right)


def joined(est_ref, mid_ref, left_ref, right_ref, q, g, head, tail):
    z = g * ZPER + q
    total = mid_ref[z] + beside(q, g, slice(RIM, RIM + SIDE), left_ref, right_ref)
    total = jnp.concatenate(
        [total[:RIM] + head, total[RIM : SIDE - RIM], total[SIDE - RIM :] + tail], axis=0
    )
    return est_ref[z] * total / VIEWS


def last_join_body(est_ref, mid_ref, left_ref, right_ref, above_ref, below_ref, out_ref):
    @pl.loop(0, ZPER, unroll=2)
    def _(q):
        for g in range(GROUPS):
            z = g * ZPER + q
            out_ref[z] = joined(
                est_ref, mid_ref, left_ref, right_ref, q, g,
                decode(above_ref[z]), decode(below_ref[z]),
            )


def last_join(est, mid, from_left, from_right, above, below):
    return pl.pallas_call(
        last_join_body,
        out_shape=jax.ShapeDtypeStruct(CORE, jnp.float32),
        compiler_params=room(20),
        name="last_join",
    )(est, mid, from_left, from_right, above, below)


def cut(q, planes, left_ref, right_ref):
    low = jnp.zeros((EXT, SIDE), jnp.float32)
    high = jnp.zeros((EXT, SIDE), jnp.float32)
    for g, plane in enumerate(planes):
        mine = lanes((EXT, SIDE)) // RIM == g
        low = jnp.where(mine, pltpu.roll(plane, RIM * g, 1), low)
        high = jnp.where(mine, pltpu.roll(plane, (RIM * g + RIM) % SIDE, 1), high)
    left_ref[q] = low.astype(jnp.bfloat16)
    right_ref[q] = high.astype(jnp.bfloat16)


def next_join_body(
    est_ref, mid_ref, left_ref, right_ref, above_ref, below_ref,
    up_ref, down_ref, top_ref, bot_ref,
    out_ref, newtop_ref, newbot_ref, goleft_ref, goright_ref,
):
    @pl.loop(0, ZPER, unroll=2)
    def _(q):
        planes = []
        for g in range(GROUPS):
            z = g * ZPER + q
            now = joined(
                est_ref, mid_ref, left_ref, right_ref, q, g,
                decode(above_ref[z]), decode(below_ref[z]),
            )
            out_ref[z] = now
            total = decode(above_ref[CZ + z]) + up_ref[z]
            newtop = top_ref[z].astype(jnp.float32) * total / VIEWS
            newtop_ref[z] = newtop.astype(jnp.bfloat16)
            total = decode(below_ref[CZ + z]) + down_ref[z]
            newbot = bot_ref[z].astype(jnp.float32) * total / VIEWS
            newbot_ref[z] = newbot.astype(jnp.bfloat16)
            planes.append(jnp.concatenate([newtop, now, newbot], axis=0))
        cut(q, planes, goleft_ref, goright_ref)


def next_join(est, mid, from_left, from_right, above, below, up, down, top, bot):
    rows = jax.ShapeDtypeStruct(ROWS, jnp.bfloat16)
    strip = jax.ShapeDtypeStruct(STRIP, jnp.bfloat16)
    return pl.pallas_call(
        next_join_body,
        out_shape=(jax.ShapeDtypeStruct(CORE, jnp.float32), rows, rows, strip, strip),
        compiler_params=room(24),
        name="next_join",
    )(est, mid, from_left, from_right, above, below, up, down, top, bot)


def rims_body(first_ref, last_ref, top_ref, bot_ref):
    top_ref[...] = first_ref[...].astype(jnp.bfloat16)
    bot_ref[...] = last_ref[...].astype(jnp.bfloat16)


def rims(est):
    rows = jax.ShapeDtypeStruct(ROWS, jnp.bfloat16)
    return pl.pallas_call(
        rims_body,
        out_shape=(rows, rows),
        grid=(1,),
        in_specs=[
            pl.BlockSpec(ROWS, lambda i: (0, 0, 0)),
            pl.BlockSpec(ROWS, lambda i: (0, SIDE // RIM - 1, 0)),
        ],
        out_specs=[whole(*ROWS), whole(*ROWS)],
        compiler_params=room(56),
        name="rims",
    )(est, est)


def edges_body(est_ref, top_ref, bot_ref, left_ref, right_ref):
    @pl.loop(0, ZPER, unroll=2)
    def _(q):
        planes = []
        for g in range(GROUPS):
            z = g * ZPER + q
            rim = (top_ref[z].astype(jnp.float32), bot_ref[z].astype(jnp.float32))
            planes.append(jnp.concatenate([rim[0], est_ref[z], rim[1]], axis=0))
        cut(q, planes, left_ref, right_ref)


def edges(est, top, bot):
    strip = jax.ShapeDtypeStruct(STRIP, jnp.bfloat16)
    return pl.pallas_call(
        edges_body,
        out_shape=(strip, strip),
        compiler_params=room(12),
        name="edges",
    )(est, top, bot)


def pick(taps, offset):
    hot = (offset[:, :, None] == jnp.arange(TAPS)[None, None, :]).astype(jnp.bfloat16)
    return jnp.einsum("rct,vt->vrc", hot, taps, preferred_element_type=jnp.float32).astype(
        jnp.bfloat16
    )


def weights_of(psf):
    kernel = (psf / jnp.sum(psf, axis=2, keepdims=True)).astype(jnp.bfloat16)
    core = jnp.arange(SIDE)
    rim = jnp.arange(RIM)
    far = jnp.full((SIDE - 2 * RIM,), 4 * SIDE)
    where_x = jnp.concatenate([core, rim - RIM, SIDE + rim, far])
    wx = pick(kernel[:, 2], where_x[:, None] - core[None, :] + REACH)
    wx = jnp.transpose(wx, (1, 0, 2)).reshape(2 * SIDE, VIEWS * SIDE)
    bx = pick(kernel[:, 2], where_x[None, :] - core[:, None] + REACH).reshape(
        VIEWS * SIDE, 2 * SIDE
    )
    where_y = jnp.arange(EXT) - RIM
    wy = pick(kernel[:, 1], where_y[None, :] - core[:, None] + REACH)
    by = pick(kernel[:, 1], where_y[:, None] - core[None, :] + REACH)
    row = jnp.arange(CZ * HALF_TILE)
    same = row[:, None] % HALF_TILE == row[None, :] % HALF_TILE
    gap = row[None, :] // HALF_TILE - row[:, None] // HALF_TILE
    wz = pick(kernel[:, 0], jnp.where(same, gap + REACH, -1))
    bz = pick(kernel[:, 0], jnp.where(same, REACH - gap, -1))
    return wx, wy, wz, bx, by, bz


def local(tiles, tile_dest, tile_slot, psf, estimate):
    axes = ("gy", "gx")
    devices = lax.axis_size("gy") * lax.axis_size("gx")
    first_rows, last_rows = rims(estimate)
    top, bot = shift(last_rows, "gy", 1), shift(first_rows, "gy", -1)
    dest = tile_dest[:, 0]
    count = dest.shape[0]
    order = (jnp.arange(count) * 256 + tile_slot)[None, :]
    hit = dest[None, :] == jnp.arange(devices)[:, None]
    first = jnp.min(jnp.where(hit, order, count * 256), axis=1)[:, None, None]
    last = jnp.max(jnp.where(hit, order, -1), axis=1)[:, None, None]
    one = jnp.where(first < count * 256, first % 256 + 1, 0)
    two = jnp.where(last > first, last % 256 + 1, 0)
    shape = (devices, HALF_TILE, SIDE)
    row = lax.broadcasted_iota(jnp.int32, shape, 1)
    mine = lanes(shape) == lax.axis_index(axes)
    labels = jnp.where(row == 0, one, jnp.where(row == 1, two, 0))
    labels = jnp.where(mine, labels, 0).astype(jnp.bfloat16)
    labels, top, bot = lax.optimization_barrier((labels, top, bot))
    low, high = edges(estimate, top, bot)
    left, right = shift(high, "gx", 1), shift(low, "gx", -1)
    packed = pack(dest, tiles, labels)
    packed, left, right = lax.optimization_barrier((packed, left, right))
    got = lax.all_to_all(packed, axes, split_axis=0, concat_axis=0, tiled=True)
    weights = weights_of(psf)
    blur = forward(estimate, (top, bot, left, right), weights)
    *parts, observed, counted = backward(got, blur, weights)
    for repeat_index in range(ITERS):
        more = repeat_index + 1 < ITERS
        mid, up, down, goleft, goright = parts
        sides = shift(goright, "gx", 1), shift(goleft, "gx", -1)
        sent = join_x(mid, up, down, *sides, more)
        if not more:
            goup, godown = sent
            return last_join(
                estimate, mid, *sides, shift(godown, "gy", 1), shift(goup, "gy", -1)
            )
        goup, godown, up, down = sent
        estimate, top, bot, low, high = next_join(
            estimate, mid, *sides, shift(godown, "gy", 1), shift(goup, "gy", -1), up, down, top, bot
        )
        halo = top, bot, shift(high, "gx", 1), shift(low, "gx", -1)
        parts = iterate(counted, estimate, halo, observed, weights)


def solution(mesh):
    placed = (
        P(("gy", "gx"), None, None),
        P(("gy", "gx"), None),
        P(("gy", "gx")),
        P(),
        P(None, "gy", "gx"),
    )
    return jax.shard_map(
        local, mesh=mesh, in_specs=placed, out_specs=P(None, "gy", "gx"), check_vma=False
    )
```

```python
import jax
import jax.numpy as jnp
from jax import lax
from jax.experimental import pallas as pl
from jax.experimental.pallas import tpu as pltpu
from jax.sharding import PartitionSpec as P

ITERS = 2
DAMPING = 0.05
VIEWS = 6
TAPS = 31
REACH = 15
CZ = 32
SIDE = 128
RIM = 16
EXT = SIDE + 2 * RIM
GROUPS = SIDE // RIM
ZPER = CZ // GROUPS
SLOTS = 2
HALF_TILE = 8
UX, UY, UZ, UB, UE = 4, 16, 8, 16, 4
def room(mebibytes):
    return pltpu.CompilerParams(vmem_limit_bytes=mebibytes << 20)


def shift(values, axis, step):
    count = lax.axis_size(axis)
    pairs = [(i, i + step) for i in range(count) if 0 <= i + step < count]
    return lax.ppermute(values, axis, pairs)


def lanes(shape):
    return lax.broadcasted_iota(jnp.int32, shape, len(shape) - 1)


def pack_body(
    dest_ref, tiles_ref, labels_ref, out_ref, held_ref, seen_ref, load_sems, tile_sem, label_sem
):
    devices = out_ref.shape[0]
    pieces = load_sems.shape[0]
    count = tiles_ref.shape[0]
    piece = count // pieces
    loads = []
    for p in range(pieces):
        part = pl.ds(p * piece, piece)
        loads.append(
            pltpu.make_async_copy(tiles_ref.at[part], held_ref.at[part], load_sems.at[p])
        )
        loads[-1].start()
    named = pltpu.make_async_copy(
        labels_ref, out_ref.at[:, pl.ds(SLOTS * SIDE, HALF_TILE)], label_sem
    )
    named.start()

    @pl.loop(0, devices, unroll=8)
    def _(i):
        seen_ref[i] = 0

    for p in range(pieces):
        loads[p].wait()

        @pl.loop(p * piece, (p + 1) * piece, unroll=4)
        def _(i):
            target = dest_ref[i]
            rank = seen_ref[target]
            seen_ref[target] = rank + 1
            pltpu.make_async_copy(
                held_ref.at[i], out_ref.at[target, pl.ds(rank * SIDE, SIDE)], tile_sem
            ).start()

    every = out_ref.at[pl.ds(0, count // SLOTS), pl.ds(0, SLOTS * SIDE)]
    pltpu.make_async_copy(every, every, tile_sem).wait()
    named.wait()


def pack(tile_dest, tiles, labels):
    devices = labels.shape[0]
    return pl.pallas_call(
        pack_body,
        out_shape=jax.ShapeDtypeStruct((devices, SLOTS * SIDE + HALF_TILE, SIDE), tiles.dtype),
        in_specs=[
            pl.BlockSpec(memory_space=pltpu.SMEM),
            pl.BlockSpec(memory_space=pl.ANY),
            pl.BlockSpec(memory_space=pltpu.VMEM),
        ],
        out_specs=pl.BlockSpec(memory_space=pltpu.HBM),
        scratch_shapes=[
            pltpu.VMEM(tiles.shape, tiles.dtype),
            pltpu.SMEM((devices,), jnp.int32),
            pltpu.SemaphoreType.DMA((4,)),
            pltpu.SemaphoreType.DMA(()),
            pltpu.SemaphoreType.DMA(()),
        ],
        compiler_params=room(56),
        name="pack",
    )(tile_dest, tiles, labels)


TOP_CODE = 32767
KNEE = 8.0


def encode(sums):
    code = (sums / (sums + KNEE) * TOP_CODE + 0.5).astype(jnp.int32)
    return jnp.minimum(code, TOP_CODE - 1).astype(jnp.int16)


def decode(codes):
    codes = codes.astype(jnp.int32).astype(jnp.float32)
    return KNEE * codes / (TOP_CODE - codes)


def side_by_side(pair):
    return jnp.concatenate([pair[:, :HALF_TILE], pair[:, HALF_TILE:]], axis=2).reshape(
        -1, 2 * SIDE
    )


def interleave(wide):
    wide = wide.reshape(-1, HALF_TILE, 2 * SIDE)
    return jnp.concatenate([wide[:, :, :SIDE], wide[:, :, SIDE:]], axis=1)


def filter_x(est_ref, top_ref, bot_ref, left_ref, right_ref, wx_ref, wide_ref, ax_ref):
    @pl.loop(0, GROUPS, unroll=UX)
    def _(g):
        z0 = g * ZPER
        slot = g % UX
        wide_ref[slot, :, RIM : RIM + SIDE, 0:SIDE] = est_ref[pl.ds(z0, ZPER)].astype(
            jnp.bfloat16
        )
        wide_ref[slot, :, 0:RIM, 0:SIDE] = top_ref[pl.ds(z0, ZPER)]
        wide_ref[slot, :, RIM + SIDE : EXT, 0:SIDE] = bot_ref[pl.ds(z0, ZPER)]
        for q in range(ZPER):
            lane = lanes((EXT, SIDE))
            lo = pltpu.roll(left_ref[q].astype(jnp.float32), (SIDE - RIM * g) % SIDE, 1)
            hi = pltpu.roll(right_ref[q].astype(jnp.float32), (SIDE + RIM - RIM * g) % SIDE, 1)
            both = jnp.where(lane < RIM, lo, jnp.where(lane < 2 * RIM, hi, 0.0))
            wide_ref[slot, q, :, SIDE : 2 * SIDE] = both.astype(jnp.bfloat16)
        for q in range(ZPER):
            got = jnp.dot(
                wide_ref[slot, q], wx_ref[...], preferred_element_type=jnp.float32
            ).astype(jnp.bfloat16)
            for w in range(VIEWS):
                ax_ref[w, z0 + q] = got[:, w * SIDE : (w + 1) * SIDE]


def filter_y(v, wy_ref, ax_ref, ay_ref):
    @pl.loop(0, CZ // 2, unroll=UY)
    def _(i):
        pair = jnp.concatenate([ax_ref[v, 2 * i], ax_ref[v, 2 * i + 1]], axis=1)
        got = jnp.dot(wy_ref[0], pair, preferred_element_type=jnp.float32)
        ay_ref[:, i] = interleave(got).astype(jnp.bfloat16)


def filter_z(i, wz_ref, ay_ref):
    one = ay_ref[2 * i].reshape(CZ * HALF_TILE, SIDE)
    two = ay_ref[2 * i + 1].reshape(CZ * HALF_TILE, SIDE)
    return jnp.dot(
        wz_ref[0], jnp.concatenate([one, two], axis=1), preferred_element_type=jnp.float32
    )


def compare(i, blur, seen, count_ref, bz_ref, rz_ref):
    rows = pl.ds(pl.multiple_of(i * RIM, RIM), RIM)
    seen = side_by_side(seen.astype(jnp.float32))
    times = jnp.concatenate([count_ref[0], count_ref[0]], axis=1)
    ratio = ((seen + DAMPING) / (times * blur + DAMPING)).astype(jnp.bfloat16)
    back = jnp.dot(bz_ref[0], ratio, preferred_element_type=jnp.float32)
    rz_ref[:, rows, :] = interleave(back).astype(jnp.bfloat16)


def spread_y(v, by_ref, rz_ref, ry_ref):
    at = pl.ds(pl.multiple_of(v * SIDE, SIDE), SIDE)

    @pl.loop(0, CZ // 2, unroll=UB)
    def _(i):
        pair = jnp.concatenate([rz_ref[2 * i], rz_ref[2 * i + 1]], axis=1)
        got = jnp.dot(by_ref[0], pair, preferred_element_type=jnp.float32).astype(jnp.bfloat16)
        ry_ref[2 * i, :, at] = got[:, :SIDE]
        ry_ref[2 * i + 1, :, at] = got[:, SIDE:]


def spread_x(bx_ref, ry_ref, mid_ref, up_ref, down_ref, goleft_ref, goright_ref):
    @pl.loop(0, ZPER, unroll=UE)
    def _(q):
        goleft = jnp.zeros((EXT, SIDE), jnp.float32)
        goright = jnp.zeros((EXT, SIDE), jnp.float32)
        for g in range(GROUPS):
            z = g * ZPER + q
            got = jnp.dot(ry_ref[z], bx_ref[...], preferred_element_type=jnp.float32)
            up_ref[z] = got[:RIM, :SIDE]
            mid_ref[z] = got[RIM : RIM + SIDE, :SIDE]
            down_ref[z] = got[RIM + SIDE :, :SIDE]
            strip = got[:, SIDE:]
            mine = lanes((EXT, SIDE)) // RIM == g
            goleft = jnp.where(mine, pltpu.roll(strip, RIM * g, 1), goleft)
            goright = jnp.where(mine, pltpu.roll(strip, (SIDE + RIM * g - RIM) % SIDE, 1), goright)
        goleft_ref[q] = encode(goleft)
        goright_ref[q] = encode(goright)


def forward_body(
    est_ref, top_ref, bot_ref, left_ref, right_ref, wx_ref, wy_ref, wz_ref,
    blur_ref, wide_ref, ax_ref, ay_ref,
):
    v = pl.program_id(0)

    @pl.when(v == 0)
    def _():
        filter_x(est_ref, top_ref, bot_ref, left_ref, right_ref, wx_ref, wide_ref, ax_ref)

    filter_y(v, wy_ref, ax_ref, ay_ref)

    @pl.loop(0, SIDE // RIM, unroll=UZ)
    def _(i):
        blur_ref[0, i] = filter_z(i, wz_ref, ay_ref)


def backward_body(
    got_ref, blur_ref, bx_ref, by_ref, bz_ref,
    mid_ref, up_ref, down_ref, goleft_ref, goright_ref, obs_ref, count_ref,
    rz_ref, ry_ref, tiles_ref, names_ref, wide_ref, label_ref, head_ref, next_ref, times_ref,
    many_ref, plane_ref, sems,
):
    v = pl.program_id(0)
    sources = got_ref.shape[0]

    @pl.when(v == 0)
    def _():
        names = pltpu.make_async_copy(
            got_ref.at[:, pl.ds(SLOTS * SIDE, HALF_TILE)], names_ref, sems.at[0]
        )
        tiles = pltpu.make_async_copy(
            got_ref.at[:, pl.ds(0, SLOTS * SIDE)], tiles_ref, sems.at[1]
        )
        names.start()
        tiles.start()

        @pl.loop(0, VIEWS * CZ, unroll=8)
        def _(i):
            head_ref[i] = 0
            times_ref[i] = 0

        head_ref[VIEWS * CZ] = 0
        times_ref[VIEWS * CZ] = 0
        for w in range(VIEWS + 1):
            many_ref[w] = 0

        names.wait()
        wide_ref[...] = jnp.sum(names_ref[...].astype(jnp.float32), axis=0).astype(jnp.int32)
        labels = pltpu.make_async_copy(wide_ref, label_ref, sems.at[2])
        labels.start()
        labels.wait()

        @pl.loop(0, sources, unroll=8)
        def _(i):
            for r in range(SLOTS):
                name = label_ref[r, i] - 1
                label = jnp.where(name < 0, VIEWS * CZ, name)
                times = times_ref[label]
                next_ref[i * SLOTS + r] = head_ref[label]
                head_ref[label] = i * SLOTS + r
                times_ref[label] = times + 1
                view = label // CZ
                many = many_ref[view]
                plane_ref[view * (CZ + 1) + many] = label
                second = (times == 1) & (name >= 0)
                many_ref[view] = many + second.astype(jnp.int32)

        tiles.wait()

    def tile(i):
        return tiles_ref[i // SLOTS, pl.ds(pl.multiple_of(i % SLOTS * SIDE, SIDE), SIDE)]

    @pl.loop(0, CZ, unroll=16)
    def _(z):
        first = head_ref[v * CZ + z]
        times = times_ref[v * CZ + z]
        count_ref[0, pl.ds(pl.multiple_of(z * HALF_TILE, HALF_TILE), HALF_TILE)] = jnp.full(
            (HALF_TILE, SIDE), times.astype(jnp.float32)
        )
        obs_ref[0, z] = jnp.where(times > 0, tile(first), jnp.zeros((), jnp.bfloat16))

    @pl.loop(0, many_ref[v])
    def _(i):
        plane = plane_ref[v * (CZ + 1) + i]

        def add(_, carry):
            at, total = carry
            return next_ref[at], total + tile(at).astype(jnp.float32)

        total = jnp.zeros((SIDE, SIDE), jnp.float32)
        total = lax.fori_loop(0, times_ref[plane], add, (head_ref[plane], total))[1]
        obs_ref[0, plane - v * CZ] = total.astype(jnp.bfloat16)

    @pl.loop(0, SIDE // RIM, unroll=UZ)
    def _(i):
        rows = pl.ds(pl.multiple_of(i * RIM, RIM), RIM)
        compare(i, blur_ref[0, i], obs_ref[0, :, rows, :], count_ref, bz_ref, rz_ref)

    spread_y(v, by_ref, rz_ref, ry_ref)

    @pl.when(v == VIEWS - 1)
    def _():
        spread_x(bx_ref, ry_ref, mid_ref, up_ref, down_ref, goleft_ref, goright_ref)


def step_body(
    est_ref, top_ref, bot_ref, left_ref, right_ref, obs_ref, count_ref,
    wx_ref, wy_ref, wz_ref, bx_ref, by_ref, bz_ref,
    mid_ref, up_ref, down_ref, goleft_ref, goright_ref,
    wide_ref, ax_ref, ay_ref, rz_ref, ry_ref,
):
    v = pl.program_id(0)

    @pl.when(v == 0)
    def _():
        filter_x(est_ref, top_ref, bot_ref, left_ref, right_ref, wx_ref, wide_ref, ax_ref)

    filter_y(v, wy_ref, ax_ref, ay_ref)

    @pl.loop(0, SIDE // RIM, unroll=UZ)
    def _(i):
        rows = pl.ds(pl.multiple_of(i * RIM, RIM), RIM)
        blur = filter_z(i, wz_ref, ay_ref)
        compare(i, blur, obs_ref[0, :, rows, :], count_ref, bz_ref, rz_ref)

    spread_y(v, by_ref, rz_ref, ry_ref)

    @pl.when(v == VIEWS - 1)
    def _():
        spread_x(bx_ref, ry_ref, mid_ref, up_ref, down_ref, goleft_ref, goright_ref)


def whole(*shape):
    return pl.BlockSpec(shape, lambda v, *_: (0,) * len(shape))


def once(*shape):
    return pl.BlockSpec(
        shape, lambda v, *_: (0,) * len(shape), pipeline_mode=pl.Buffered(1)
    )


def per_view(*shape):
    return pl.BlockSpec((1,) + shape, lambda v, *_: (v,) + (0,) * len(shape))


ROWS = (CZ, RIM, SIDE)
CORE = (CZ, SIDE, SIDE)
STRIP = (ZPER, EXT, SIDE)
Z_BAND = (CZ * HALF_TILE, CZ * HALF_TILE)
TIMES = (CZ * HALF_TILE, SIDE)
BLUR = (SIDE // RIM, CZ * HALF_TILE, 2 * SIDE)
HALO_SPECS = [once(*ROWS), once(*ROWS), once(*STRIP), once(*STRIP)]
FRONT_SPECS = [once(2 * SIDE, VIEWS * SIDE), per_view(SIDE, EXT), per_view(*Z_BAND)]
BACK_SPECS = [once(VIEWS * SIDE, 2 * SIDE), per_view(EXT, SIDE), per_view(*Z_BAND)]
PART_SPECS = [whole(*CORE), whole(*ROWS), whole(*ROWS), whole(*STRIP), whole(*STRIP)]
PARTS = tuple(jax.ShapeDtypeStruct(shape, jnp.float32) for shape in (CORE, ROWS, ROWS)) + (
    jax.ShapeDtypeStruct(STRIP, jnp.int16),
    jax.ShapeDtypeStruct(STRIP, jnp.int16),
)
FRONT_SCRATCH = [
    pltpu.VMEM((UX, ZPER, EXT, 2 * SIDE), jnp.bfloat16),
    pltpu.VMEM((VIEWS, CZ, EXT, SIDE), jnp.bfloat16),
    pltpu.VMEM((SIDE // HALF_TILE, CZ // 2, RIM, SIDE), jnp.bfloat16),
]
BACK_SCRATCH = [
    pltpu.VMEM(CORE, jnp.bfloat16),
    pltpu.VMEM((CZ, EXT, VIEWS * SIDE), jnp.bfloat16),
]


def forward(est, halo, weights):
    return pl.pallas_call(
        forward_body,
        out_shape=jax.ShapeDtypeStruct((VIEWS,) + BLUR, jnp.float32),
        grid=(VIEWS,),
        in_specs=[once(*CORE)] + HALO_SPECS + FRONT_SPECS,
        out_specs=per_view(*BLUR),
        scratch_shapes=FRONT_SCRATCH,
        compiler_params=room(30),
        name="forward",
    )(est, *halo, *weights[:3])


def backward(got, blur, weights):
    sources = got.shape[0]
    return pl.pallas_call(
        backward_body,
        out_shape=PARTS
        + (
            jax.ShapeDtypeStruct((VIEWS,) + CORE, jnp.bfloat16),
            jax.ShapeDtypeStruct((VIEWS,) + TIMES, jnp.float32),
        ),
        grid=(VIEWS,),
        in_specs=[pl.BlockSpec(memory_space=pl.ANY), per_view(*BLUR)] + BACK_SPECS,
        out_specs=PART_SPECS + [per_view(*CORE), per_view(*TIMES)],
        scratch_shapes=BACK_SCRATCH
        + [
            pltpu.VMEM((sources, SLOTS * SIDE, SIDE), jnp.bfloat16),
            pltpu.VMEM((sources, HALF_TILE, SIDE), jnp.bfloat16),
            pltpu.VMEM((HALF_TILE, SIDE), jnp.int32),
            pltpu.SMEM((HALF_TILE, SIDE), jnp.int32),
            pltpu.SMEM((VIEWS * CZ + 1,), jnp.int32),
            pltpu.SMEM((sources * SLOTS,), jnp.int32),
            pltpu.SMEM((VIEWS * CZ + 1,), jnp.int32),
            pltpu.SMEM((VIEWS + 1,), jnp.int32),
            pltpu.SMEM(((VIEWS + 1) * (CZ + 1),), jnp.int32),
            pltpu.SemaphoreType.DMA((3,)),
        ],
        compiler_params=room(38),
        name="backward",
    )(got, blur, *weights[3:])


def iterate(counted, est, halo, observed, weights):
    return pl.pallas_call(
        step_body,
        out_shape=PARTS,
        grid=(VIEWS,),
        in_specs=[once(*CORE)]
        + HALO_SPECS
        + [per_view(*CORE), per_view(*TIMES)]
        + FRONT_SPECS
        + BACK_SPECS,
        out_specs=PART_SPECS,
        scratch_shapes=FRONT_SCRATCH + BACK_SCRATCH,
        compiler_params=room(38),
        name="iterate",
    )(est, *halo, observed, counted, *weights)


def beside(q, g, rows, left_ref, right_ref):
    low = pltpu.roll(decode(left_ref[q, rows]), (SIDE - RIM * g) % SIDE, 1)
    high = pltpu.roll(decode(right_ref[q, rows]), (2 * SIDE - RIM - RIM * g) % SIDE, 1)
    lane = lanes(low.shape)
    return jnp.where(lane < RIM, low, jnp.where(lane >= SIDE - RIM, high, 0.0))


def join_x_body(first_ref, last_ref, up_ref, down_ref, left_ref, right_ref, *outs):
    goup_ref, godown_ref = outs[:2]

    @pl.loop(0, ZPER, unroll=True)
    def _(q):
        for g in range(GROUPS):
            z = g * ZPER + q
            head = up_ref[z] + beside(q, g, slice(0, RIM), left_ref, right_ref)
            tail = down_ref[z] + beside(q, g, slice(SIDE + RIM, EXT), left_ref, right_ref)
            goup_ref[z], godown_ref[z] = encode(head), encode(tail)
            if len(outs) > 2:
                outs[2][z], outs[3][z] = head, tail
                own = first_ref[z] + beside(q, g, slice(RIM, 2 * RIM), left_ref, right_ref)
                goup_ref[CZ + z] = encode(own)
                own = last_ref[z] + beside(q, g, slice(SIDE, SIDE + RIM), left_ref, right_ref)
                godown_ref[CZ + z] = encode(own)


def join_x(mid, up, down, from_left, from_right, more):
    rows = jax.ShapeDtypeStruct(ROWS, jnp.float32)
    message = jax.ShapeDtypeStruct(((1 + more) * CZ, RIM, SIDE), jnp.int16)
    out_shape = (message, message) + ((rows, rows) if more else ())
    return pl.pallas_call(
        join_x_body,
        out_shape=out_shape,
        grid=(1,),
        in_specs=[
            pl.BlockSpec(ROWS, lambda i: (0, 0, 0)),
            pl.BlockSpec(ROWS, lambda i: (0, SIDE // RIM - 1, 0)),
            whole(*ROWS),
            whole(*ROWS),
            whole(*STRIP),
            whole(*STRIP),
        ],
        out_specs=[whole(*shape.shape) for shape in out_shape],
        compiler_params=room(12),
        name="join_x",
    )(mid, mid, up, down, from_left, from_right)


def joined(est_ref, mid_ref, left_ref, right_ref, q, g, head, tail):
    z = g * ZPER + q
    total = mid_ref[z] + beside(q, g, slice(RIM, RIM + SIDE), left_ref, right_ref)
    total = jnp.concatenate(
        [total[:RIM] + head, total[RIM : SIDE - RIM], total[SIDE - RIM :] + tail], axis=0
    )
    return est_ref[z] * total / VIEWS


def last_join_body(est_ref, mid_ref, left_ref, right_ref, above_ref, below_ref, out_ref):
    @pl.loop(0, ZPER, unroll=2)
    def _(q):
        for g in range(GROUPS):
            z = g * ZPER + q
            out_ref[z] = joined(
                est_ref, mid_ref, left_ref, right_ref, q, g,
                decode(above_ref[z]), decode(below_ref[z]),
            )


def last_join(est, mid, from_left, from_right, above, below):
    return pl.pallas_call(
        last_join_body,
        out_shape=jax.ShapeDtypeStruct(CORE, jnp.float32),
        compiler_params=room(20),
        name="last_join",
    )(est, mid, from_left, from_right, above, below)


def cut(q, planes, left_ref, right_ref):
    low = jnp.zeros((EXT, SIDE), jnp.float32)
    high = jnp.zeros((EXT, SIDE), jnp.float32)
    for g, plane in enumerate(planes):
        mine = lanes((EXT, SIDE)) // RIM == g
        low = jnp.where(mine, pltpu.roll(plane, RIM * g, 1), low)
        high = jnp.where(mine, pltpu.roll(plane, (RIM * g + RIM) % SIDE, 1), high)
    left_ref[q] = low.astype(jnp.bfloat16)
    right_ref[q] = high.astype(jnp.bfloat16)


def next_join_body(
    est_ref, mid_ref, left_ref, right_ref, above_ref, below_ref,
    up_ref, down_ref, top_ref, bot_ref,
    out_ref, newtop_ref, newbot_ref, goleft_ref, goright_ref,
):
    @pl.loop(0, ZPER, unroll=2)
    def _(q):
        planes = []
        for g in range(GROUPS):
            z = g * ZPER + q
            now = joined(
                est_ref, mid_ref, left_ref, right_ref, q, g,
                decode(above_ref[z]), decode(below_ref[z]),
            )
            out_ref[z] = now
            total = decode(above_ref[CZ + z]) + up_ref[z]
            newtop = top_ref[z].astype(jnp.float32) * total / VIEWS
            newtop_ref[z] = newtop.astype(jnp.bfloat16)
            total = decode(below_ref[CZ + z]) + down_ref[z]
            newbot = bot_ref[z].astype(jnp.float32) * total / VIEWS
            newbot_ref[z] = newbot.astype(jnp.bfloat16)
            planes.append(jnp.concatenate([newtop, now, newbot], axis=0))
        cut(q, planes, goleft_ref, goright_ref)


def next_join(est, mid, from_left, from_right, above, below, up, down, top, bot):
    rows = jax.ShapeDtypeStruct(ROWS, jnp.bfloat16)
    strip = jax.ShapeDtypeStruct(STRIP, jnp.bfloat16)
    return pl.pallas_call(
        next_join_body,
        out_shape=(jax.ShapeDtypeStruct(CORE, jnp.float32), rows, rows, strip, strip),
        compiler_params=room(24),
        name="next_join",
    )(est, mid, from_left, from_right, above, below, up, down, top, bot)


def rims_body(first_ref, last_ref, top_ref, bot_ref):
    top_ref[...] = first_ref[...].astype(jnp.bfloat16)
    bot_ref[...] = last_ref[...].astype(jnp.bfloat16)


def rims(est):
    rows = jax.ShapeDtypeStruct(ROWS, jnp.bfloat16)
    return pl.pallas_call(
        rims_body,
        out_shape=(rows, rows),
        grid=(1,),
        in_specs=[
            pl.BlockSpec(ROWS, lambda i: (0, 0, 0)),
            pl.BlockSpec(ROWS, lambda i: (0, SIDE // RIM - 1, 0)),
        ],
        out_specs=[whole(*ROWS), whole(*ROWS)],
        compiler_params=room(56),
        name="rims",
    )(est, est)


def edges_body(est_ref, top_ref, bot_ref, left_ref, right_ref):
    @pl.loop(0, ZPER, unroll=2)
    def _(q):
        planes = []
        for g in range(GROUPS):
            z = g * ZPER + q
            rim = (top_ref[z].astype(jnp.float32), bot_ref[z].astype(jnp.float32))
            planes.append(jnp.concatenate([rim[0], est_ref[z], rim[1]], axis=0))
        cut(q, planes, left_ref, right_ref)


def edges(est, top, bot):
    strip = jax.ShapeDtypeStruct(STRIP, jnp.bfloat16)
    return pl.pallas_call(
        edges_body,
        out_shape=(strip, strip),
        compiler_params=room(12),
        name="edges",
    )(est, top, bot)


def pick(taps, offset):
    hot = (offset[:, :, None] == jnp.arange(TAPS)[None, None, :]).astype(jnp.bfloat16)
    return jnp.einsum("rct,vt->vrc", hot, taps, preferred_element_type=jnp.float32).astype(
        jnp.bfloat16
    )


def weights_of(psf):
    kernel = (psf / jnp.sum(psf, axis=2, keepdims=True)).astype(jnp.bfloat16)
    core = jnp.arange(SIDE)
    rim = jnp.arange(RIM)
    far = jnp.full((SIDE - 2 * RIM,), 4 * SIDE)
    where_x = jnp.concatenate([core, rim - RIM, SIDE + rim, far])
    wx = pick(kernel[:, 2], where_x[:, None] - core[None, :] + REACH)
    wx = jnp.transpose(wx, (1, 0, 2)).reshape(2 * SIDE, VIEWS * SIDE)
    bx = pick(kernel[:, 2], where_x[None, :] - core[:, None] + REACH).reshape(
        VIEWS * SIDE, 2 * SIDE
    )
    where_y = jnp.arange(EXT) - RIM
    wy = pick(kernel[:, 1], where_y[None, :] - core[:, None] + REACH)
    by = pick(kernel[:, 1], where_y[:, None] - core[None, :] + REACH)
    row = jnp.arange(CZ * HALF_TILE)
    same = row[:, None] % HALF_TILE == row[None, :] % HALF_TILE
    gap = row[None, :] // HALF_TILE - row[:, None] // HALF_TILE
    wz = pick(kernel[:, 0], jnp.where(same, gap + REACH, -1))
    bz = pick(kernel[:, 0], jnp.where(same, REACH - gap, -1))
    return wx, wy, wz, bx, by, bz


def local(tiles, tile_dest, tile_slot, psf, estimate):
    axes = ("gy", "gx")
    devices = lax.axis_size("gy") * lax.axis_size("gx")
    first_rows, last_rows = rims(estimate)
    top, bot = shift(last_rows, "gy", 1), shift(first_rows, "gy", -1)
    dest = tile_dest[:, 0]
    count = dest.shape[0]
    order = (jnp.arange(count) * 256 + tile_slot)[None, :]
    hit = dest[None, :] == jnp.arange(devices)[:, None]
    first = jnp.min(jnp.where(hit, order, count * 256), axis=1)[:, None, None]
    last = jnp.max(jnp.where(hit, order, -1), axis=1)[:, None, None]
    one = jnp.where(first < count * 256, first % 256 + 1, 0)
    two = jnp.where(last > first, last % 256 + 1, 0)
    shape = (devices, HALF_TILE, SIDE)
    row = lax.broadcasted_iota(jnp.int32, shape, 1)
    mine = lanes(shape) == lax.axis_index(axes)
    labels = jnp.where(row == 0, one, jnp.where(row == 1, two, 0))
    labels = jnp.where(mine, labels, 0).astype(jnp.bfloat16)
    labels, top, bot = lax.optimization_barrier((labels, top, bot))
    low, high = edges(estimate, top, bot)
    left, right = shift(high, "gx", 1), shift(low, "gx", -1)
    packed = pack(dest, tiles, labels)
    packed, left, right = lax.optimization_barrier((packed, left, right))
    got = lax.all_to_all(packed, axes, split_axis=0, concat_axis=0, tiled=True)
    weights = weights_of(psf)
    blur = forward(estimate, (top, bot, left, right), weights)
    *parts, observed, counted = backward(got, blur, weights)
    for repeat_index in range(ITERS):
        more = repeat_index + 1 < ITERS
        mid, up, down, goleft, goright = parts
        sides = shift(goright, "gx", 1), shift(goleft, "gx", -1)
        sent = join_x(mid, up, down, *sides, more)
        if not more:
            goup, godown = sent
            return last_join(
                estimate, mid, *sides, shift(godown, "gy", 1), shift(goup, "gy", -1)
            )
        goup, godown, up, down = sent
        estimate, top, bot, low, high = next_join(
            estimate, mid, *sides, shift(godown, "gy", 1), shift(goup, "gy", -1), up, down, top, bot
        )
        halo = top, bot, shift(high, "gx", 1), shift(low, "gx", -1)
        parts = iterate(counted, estimate, halo, observed, weights)


def solution(mesh):
    placed = (
        P(("gy", "gx"), None, None),
        P(("gy", "gx"), None),
        P(("gy", "gx")),
        P(),
        P(None, "gy", "gx"),
    )
    return jax.shard_map(
        local, mesh=mesh, in_specs=placed, out_specs=P(None, "gy", "gx"), check_vma=False
    )
```
